512 devices in a mesh: batch: 128 (over x, z, y_hi), mp: 4 (over y_lo, core).
Axes of the slice: x: 4, y: 8 (y_hi: 4, y_lo: 2; y = y_hi * 2 + y_lo), z: 8, core: 2. Of those that a mesh axis runs over, the one named last changes fastest.
Arguments:
- query_hidden: bfloat16 [131072, 768], P(('batch', 'mp')), may hold values from -28 to 28
- passage_hidden: bfloat16 [655360, 768], P(('batch', 'mp')), may hold values from -28 to 28
- projection: bfloat16 [768, 128], replicated, may hold values from -0.21875 to 0.21875
- query_lengths: int32 [4096], P(('batch', 'mp')), may hold values from 8 to 32, as said below
- passage_lengths: int32 [5120], P(('batch', 'mp')), may hold values from 64 to 128, as said below
- positives: int32 [4096], P(('batch', 'mp')), may hold values from 0 to 9
Outputs:
- query_loss: float32 [4096], P(('batch', 'mp'))
- grad_query_hidden: bfloat16 [131072, 768], P(('batch', 'mp'))
- grad_passage_hidden: bfloat16 [655360, 768], P(('batch', 'mp'))
- grad_projection: float32 [768, 128], replicated
The draws below stay inside these ranges and needn't reach their ends.
Inputs may be any that keep to these rules, and one draw needn't show every extreme that they name: `query_lengths`: the first query of each block of 8 queries has all 32 tokens. `passage_lengths`: the first passage of each block of 10 passages has all 128 tokens.
All inputs are finite; a program needn't handle non-finite values.
Results may differ from the reference program's by a relative error of at most 0.012.
The reference program's roundings to bfloat16 on the way (of `query_embed`, `passage_embed`, `grad_sim`, `query_pre_grad` and `passage_pre_grad`) count: a program that leaves them out, or rounds other values in their place, can miss the bound.
Values may be sent and summed in bfloat16 or wider, within the bound.
A program may use at most 64 MiB of HBM per device.

```python
import jax
import jax.numpy as jnp
from jax import lax

H = 768
DIM = 128
QL = 32
PL = 128
BQ = 8
BP = 10
BLOCKS = 512
STRIDE = 4
NQ = 4096
NP = 5120
N_BATCH = 128
N_MP = 4


def query_rows(key):
    rows = NQ * QL
    noise = jnp.clip(jax.random.normal(jax.random.fold_in(key, 101), (rows, H), jnp.float32), -4.0, 4.0)
    return noise


def draw_query_hidden(key, part):
    values = query_rows(key)
    return values.astype(jnp.bfloat16)


def draw_passage_hidden(key, part):
    rows = NP * PL
    noise = jnp.clip(jax.random.normal(jax.random.fold_in(key, 201), (rows, H), jnp.float32), -4.0, 4.0)
    values = noise
    return values.astype(jnp.bfloat16)


def draw_query_lengths(key, part):
    lengths = jax.random.randint(jax.random.fold_in(key, 301), (NQ // BQ, BQ), QL // 4, QL + 1, jnp.int32)
    lengths = lengths.at[:, 0].set(QL)
    return lengths.reshape(NQ)


def draw_passage_lengths(key, part):
    lengths = jax.random.randint(jax.random.fold_in(key, 302), (NP // BP, BP), PL // 2, PL + 1, jnp.int32)
    lengths = lengths.at[:, 0].set(PL)
    return lengths.reshape(NP)


def place_ends(result, own_key, low, high):
    longest = result.shape.index(max(result.shape))
    spots = []
    for shift in (0, 1):
        where = [jax.random.randint(jax.random.fold_in(own_key, axis), (), 0, length) for axis, length in enumerate(result.shape)]
        where[longest] = (where[longest] + shift) % result.shape[longest]
        spots.append(tuple(where))
    return result.at[spots[0]].set(low).at[spots[1]].set(high)


def bell_draw(own_key, shape, spread, bound, held_as=jnp.bfloat16):
    drawn = jax.random.normal(own_key, shape, jnp.float32) * spread
    return jnp.minimum(jnp.maximum(drawn, -bound), bound).astype(held_as)


def setup_inputs(seed: int = 0) -> dict:
    keys = jax.random.split(jax.random.key(seed), 7)
    query_hidden = draw_query_hidden(jax.random.fold_in(keys[6], 71), 0)
    passage_hidden = draw_passage_hidden(jax.random.fold_in(keys[6], 71), 0)
    projection = bell_draw(keys[2], (H, DIM), H ** -0.5, 0.21875)
    query_lengths = draw_query_lengths(jax.random.fold_in(keys[6], 71), 0)
    passage_lengths = draw_passage_lengths(jax.random.fold_in(keys[6], 71), 0)
    positives = place_ends(jax.random.randint(keys[5], (NQ,), 0, BP), jax.random.fold_in(keys[5], 1), 0, BP - 1).astype(jnp.int32)
    return {"query_hidden": query_hidden, "passage_hidden": passage_hidden, "projection": projection, "query_lengths": query_lengths, "passage_lengths": passage_lengths, "positives": positives}


inner_scale = 128.0
outer_scale = 8.0
loss_scale = 32.0
norm_eps = 1e-06

def embed_rows(hidden, projection):
    before = jnp.dot(hidden, projection, preferred_element_type=jnp.float32)
    radius = jnp.sqrt(lax.optimization_barrier(jnp.sum(before * before, axis=-1, keepdims=True)) + norm_eps)
    return (before / radius, radius)

def candidate_block(query_embed, passage_embed, passage_valid, query_keep):
    queries, query_tokens = query_keep.shape
    passages, passage_tokens = passage_valid.shape
    sims = jnp.dot(query_embed, passage_embed.T, preferred_element_type=jnp.float32)
    sims = sims.reshape(queries, query_tokens, passages, passage_tokens)
    logits = jnp.where(passage_valid[None, None], sims * inner_scale, -jnp.inf)
    row_top = lax.optimization_barrier(jnp.max(logits, axis=-1, keepdims=True))
    powers = jnp.exp(logits - row_top)
    totals = lax.optimization_barrier(jnp.sum(powers, axis=-1, keepdims=True))
    weights = powers / totals
    best = (jnp.log(totals[..., 0]) + row_top[..., 0]) / inner_scale
    scores = outer_scale * lax.optimization_barrier(jnp.sum(query_keep[:, :, None] * best, axis=1))
    return (scores, weights)

def softmax_loss(scores, positives):
    row_top = lax.optimization_barrier(jnp.max(scores, axis=1, keepdims=True))
    totals = lax.optimization_barrier(jnp.sum(jnp.exp(scores - row_top), axis=1, keepdims=True))
    log_total = row_top + jnp.log(totals)
    probs = jnp.exp(scores - log_total)
    columns = jnp.arange(scores.shape[1], dtype=jnp.int32)
    onehot = (columns[None, :] == positives[:, None]).astype(jnp.float32)
    losses = log_total[:, 0] - lax.optimization_barrier(jnp.sum(onehot * scores, axis=1))
    return (losses, loss_scale * (probs - onehot))

def block_grads(dscores, query_keep, weights, query_embed, passage_embed):
    grad_sim = (outer_scale * dscores[:, None, :, None] * query_keep[:, :, None, None] * weights).astype(jnp.bfloat16)
    flat = grad_sim.reshape(query_embed.shape[0], passage_embed.shape[0])
    to_query = jnp.dot(flat, passage_embed, preferred_element_type=jnp.float32)
    to_passage = lax.dot_general(flat, query_embed, (((0,), (0,)), ((), ())), preferred_element_type=jnp.float32)
    return (to_query, to_passage)

def back_norm(grad, unit, radius):
    return ((grad - unit * lax.optimization_barrier(jnp.sum(unit * grad, axis=-1, keepdims=True))) / radius).astype(jnp.bfloat16)

def contract_rows(left, right):
    return lax.dot_general(left, right, (((0,), (0,)), ((), ())), preferred_element_type=jnp.float32)

def reference(query_hidden, passage_hidden, projection, query_lengths, passage_lengths, positives):
    query_unit, query_radius = embed_rows(query_hidden, projection)
    passage_unit, passage_radius = embed_rows(passage_hidden, projection)
    query_embed = query_unit.astype(jnp.bfloat16).reshape(BLOCKS, BQ * QL, DIM)
    passage_embed = passage_unit.astype(jnp.bfloat16).reshape(BLOCKS, BP * PL, DIM)
    block_lengths = passage_lengths.reshape(BLOCKS, BP)
    windows = [jnp.roll(passage_embed, -column * STRIDE, axis=0) for column in range(3)]
    window_lengths = [jnp.roll(block_lengths, -column * STRIDE, axis=0) for column in range(3)]

    def one_block(items):
        query_block, first, second, third, len_first, len_second, len_third, lengths_block, positive_block = items
        query_keep = (jnp.arange(QL, dtype=jnp.int32)[None, :] < lengths_block[:, None]).astype(jnp.float32)
        slots = jnp.arange(PL, dtype=jnp.int32)
        members = [(first, len_first), (second, len_second), (third, len_third)]
        score_list = []
        weight_list = []
        for member in members:
            valid = slots[None, :] < member[1][:, None]
            scores, weights = candidate_block(query_block, member[0], valid, query_keep)
            score_list.append(scores)
            weight_list.append(weights)
        losses, dscores = softmax_loss(jnp.concatenate(score_list, axis=1), positive_block)
        query_grad = jnp.zeros((BQ * QL, DIM), jnp.float32)
        passage_terms = []
        for column in range(3):
            to_query, to_passage = block_grads(dscores[:, column * BP:(column + 1) * BP], query_keep, weight_list[column], query_block, members[column][0])
            query_grad = query_grad + to_query
            passage_terms.append(to_passage)
        return (query_grad, jnp.stack(passage_terms), losses)
    query_grad, terms, losses = lax.map(one_block, (query_embed, windows[0], windows[1], windows[2], window_lengths[0], window_lengths[1], window_lengths[2], query_lengths.reshape(BLOCKS, BQ), positives.reshape(BLOCKS, BQ)))
    passage_grad = terms[:, 0] + jnp.roll(terms[:, 1], STRIDE, axis=0) + jnp.roll(terms[:, 2], 2 * STRIDE, axis=0)
    query_pre_grad = back_norm(query_grad.reshape(NQ * QL, DIM), query_unit, query_radius)
    passage_pre_grad = back_norm(passage_grad.reshape(NP * PL, DIM), passage_unit, passage_radius)
    grad_query_hidden = jnp.dot(query_pre_grad, projection.T, preferred_element_type=jnp.float32).astype(jnp.bfloat16)
    grad_passage_hidden = jnp.dot(passage_pre_grad, projection.T, preferred_element_type=jnp.float32).astype(jnp.bfloat16)
    grad_projection = (contract_rows(query_hidden, query_pre_grad) + contract_rows(passage_hidden, passage_pre_grad)) / (N_BATCH * N_MP)
    return (losses.reshape(NQ), grad_query_hidden, grad_passage_hidden, grad_projection)
```

```python
import functools

import jax
import jax.numpy as jnp
from jax import lax
from jax.experimental import pallas as pl
from jax.experimental.pallas import tpu as pltpu
from jax.sharding import PartitionSpec as P

inner_scale = 128.0
outer_scale = 8.0
loss_scale = 32.0
norm_eps = 1e-06

NX, NZ, NYH, NMP = 4, 8, 4, 4
NG = NYH * NMP
MESH = pl.DeviceIdType.MESH


def shifted(block, distance):
    count = NX * NZ * NYH
    return lax.ppermute(block, "batch", [(i, (i + distance) % count) for i in range(count)])


def reduce_kernel(src, out, r1, b2, b3, g4, s1, q1, s2, q2, s3, q3, s4, q4):
    bi = lax.axis_index("batch")
    mi = lax.axis_index("mp")
    yh = bi % NYH
    z = (bi // NYH) % NZ
    x = bi // (NYH * NZ)
    g = yh * NMP + mi
    rows = src.shape[0] // NG

    def group_peer(o):
        j = (g + o) % NG
        return j, (bi - yh + j // NMP, j % NMP)

    def z_peer(o):
        j = (z + o) % NZ
        return j, (x * (NZ * NYH) + j * NYH + yh, mi)

    def x_peer(o):
        j = (x + o) % NX
        return j, (j * (NZ * NYH) + z * NYH + yh, mi)

    barrier = pltpu.get_barrier_semaphore()
    for count, peer in ((NG, group_peer), (NZ, z_peer), (NX, x_peer)):
        @pl.loop(1, count)
        def _(o):
            pl.semaphore_signal(barrier, inc=1, device_id=peer(o)[1], device_id_type=MESH)
    pl.semaphore_wait(barrier, NG + NZ + NX - 3)

    def piece(j):
        return pl.ds(pl.multiple_of(j * rows, rows), rows)

    def exchange(count, peer, source, target, mine, send, recv):
        def copy(o):
            j, where = peer(o)
            return pltpu.make_async_remote_copy(
                src_ref=source(j), dst_ref=target(mine), send_sem=send.at[o], recv_sem=recv.at[mine],
                device_id=where, device_id_type=MESH)

        def arrival(o):
            j, where = peer(o)
            return pltpu.make_async_remote_copy(
                src_ref=source(j), dst_ref=target(j), send_sem=send.at[o], recv_sem=recv.at[j],
                device_id=where, device_id_type=MESH)

        @pl.loop(1, count)
        def _(o):
            copy(o).start()

        @pl.loop(1, count)
        def _(o):
            arrival(o).wait_recv()

        @pl.loop(1, count)
        def _(o):
            copy(o).wait_send()

    r1[g] = src[piece(g), :]
    exchange(NG, group_peer, lambda j: src.at[piece(j)], lambda j: r1.at[j], g, s1, q1)
    b2[z] = jnp.sum(r1[...].astype(jnp.float32), axis=0).astype(jnp.bfloat16)
    exchange(NZ, z_peer, lambda j: b2.at[z], lambda j: b2.at[j], z, s2, q2)
    b3[x] = jnp.sum(b2[...].astype(jnp.float32), axis=0).astype(jnp.bfloat16)
    exchange(NX, x_peer, lambda j: b3.at[x], lambda j: b3.at[j], x, s3, q3)
    g4[piece(g), :] = jnp.sum(b3[...].astype(jnp.float32), axis=0).astype(jnp.bfloat16)
    exchange(NG, group_peer, lambda j: g4.at[piece(g)], lambda j: g4.at[piece(j)], g, s4, q4)
    out[...] = g4[...].astype(jnp.float32) * (1.0 / (NX * NZ * NYH * NMP))


def reduce_all(partial):
    rows, dim = partial.shape
    part = rows // NG
    dma = pltpu.SemaphoreType.DMA
    return pl.pallas_call(
        reduce_kernel,
        out_shape=jax.ShapeDtypeStruct((rows, dim), jnp.float32),
        in_specs=[pl.BlockSpec(memory_space=pltpu.VMEM)],
        out_specs=pl.BlockSpec(memory_space=pltpu.VMEM),
        scratch_shapes=[
            pltpu.VMEM((NG, part, dim), jnp.bfloat16),
            pltpu.VMEM((NZ, part, dim), jnp.bfloat16),
            pltpu.VMEM((NX, part, dim), jnp.bfloat16),
            pltpu.VMEM((rows, dim), jnp.bfloat16),
            dma((NG,)), dma((NG,)), dma((NZ,)), dma((NZ,)), dma((NX,)), dma((NX,)), dma((NG,)), dma((NG,)),
        ],
        compiler_params=pltpu.CompilerParams(collective_id=0, has_side_effects=True),
    )(partial)


def embed_rows(hidden, projection):
    before = jnp.dot(hidden, projection, preferred_element_type=jnp.float32)
    radius = jnp.sqrt(jnp.sum(before * before, axis=-1, keepdims=True) + norm_eps)
    return (before / radius, radius)


def candidate_block(query_embed, passage_embed, passage_valid, query_keep):
    queries, query_tokens = query_keep.shape
    passages, passage_tokens = passage_valid.shape
    sims = jnp.dot(query_embed, passage_embed.T, preferred_element_type=jnp.float32)
    sims = sims.reshape(queries, query_tokens, passages, passage_tokens)
    logits = jnp.where(passage_valid[None, None], sims * inner_scale, -jnp.inf)
    row_top = jnp.max(logits, axis=-1, keepdims=True)
    powers = jnp.exp(logits - row_top)
    totals = jnp.sum(powers, axis=-1, keepdims=True)
    weights = powers / totals
    best = (jnp.log(totals[..., 0]) + row_top[..., 0]) / inner_scale
    scores = outer_scale * jnp.sum(query_keep[:, :, None] * best, axis=1)
    return (scores, weights)


def back_norm(grad, unit, radius):
    return ((grad - unit * jnp.sum(unit * grad, axis=-1, keepdims=True)) / radius).astype(
        jnp.bfloat16
    )


def contract_rows(left, right):
    return lax.dot_general(
        left, right, (((0,), (0,)), ((), ())), preferred_element_type=jnp.float32
    )


def per_device(query_hidden, passage_hidden, projection, query_lengths, passage_lengths, positives):
    queries = query_lengths.shape[0]
    passages = passage_lengths.shape[0]
    query_tokens = query_hidden.shape[0] // queries
    passage_tokens = passage_hidden.shape[0] // passages
    query_unit, query_radius = embed_rows(query_hidden, projection)
    query_embed = query_unit.astype(jnp.bfloat16)
    dim = query_embed.shape[1]
    packed = jnp.concatenate(
        [query_embed, jnp.broadcast_to(query_lengths.astype(jnp.bfloat16)[:, None], (queries, dim))], axis=0)
    members = [packed, shifted(packed, 1), shifted(packed, 2)]
    passage_unit, passage_radius = embed_rows(passage_hidden, projection)
    passage_embed = passage_unit.astype(jnp.bfloat16)
    slots = jnp.arange(passage_tokens, dtype=jnp.int32)
    valid = slots[None, :] < passage_lengths[:, None]
    token = jnp.arange(query_tokens, dtype=jnp.float32)
    keeps, embeds, score_list, weight_list = [], [], [], []
    for member in members:
        embed = member[:queries * query_tokens]
        keep = (token[None, :] < member[queries * query_tokens:, :1].astype(jnp.float32)).astype(jnp.float32)
        scores, weights = candidate_block(embed, passage_embed, valid, keep)
        keeps.append(keep)
        embeds.append(embed)
        score_list.append(scores)
        weight_list.append(weights)
    scores = jnp.concatenate(
        [score_list[0], shifted(score_list[1], -1), shifted(score_list[2], -2)], axis=1)
    row_top = jnp.max(scores, axis=1, keepdims=True)
    log_total = row_top + jnp.log(jnp.sum(jnp.exp(scores - row_top), axis=1, keepdims=True))
    columns = jnp.arange(passages, dtype=jnp.int32)
    onehot = (columns[None, :] == positives[:, None]).astype(jnp.float32)
    losses = log_total[:, 0] - jnp.sum(onehot * scores[:, :passages], axis=1)
    log_totals = [log_total, shifted(log_total, 1), shifted(log_total, 2)]
    flats = []
    for b in range(3):
        dscores = jnp.exp(score_list[b] - log_totals[b])
        if b == 0:
            dscores = dscores - onehot
        dscores = loss_scale * dscores
        grad_sim = (
            outer_scale * dscores[:, None, :, None] * keeps[b][:, :, None, None] * weight_list[b]
        ).astype(jnp.bfloat16)
        flats.append(grad_sim.reshape(queries * query_tokens, passages * passage_tokens))
    to_query = [jnp.dot(flat, passage_embed, preferred_element_type=jnp.float32) for flat in flats]
    back1 = shifted(to_query[1].astype(jnp.bfloat16), -1)
    back2 = shifted(to_query[2].astype(jnp.bfloat16), -2)
    passage_grad = sum(contract_rows(flat, embed) for flat, embed in zip(flats, embeds))
    passage_pre_grad = back_norm(passage_grad, passage_unit, passage_radius)
    grad_passage_hidden = jnp.dot(
        passage_pre_grad, projection.T, preferred_element_type=jnp.float32
    ).astype(jnp.bfloat16)
    passage_partial = contract_rows(passage_hidden, passage_pre_grad)
    query_grad = to_query[0] + back1.astype(jnp.float32) + back2.astype(jnp.float32)
    query_pre_grad = back_norm(query_grad, query_unit, query_radius)
    query_partial = contract_rows(query_hidden, query_pre_grad)
    grad_query_hidden = jnp.dot(
        query_pre_grad, projection.T, preferred_element_type=jnp.float32
    ).astype(jnp.bfloat16)
    grad_projection = reduce_all((query_partial + passage_partial).astype(jnp.bfloat16))
    return (losses, grad_query_hidden, grad_passage_hidden, grad_projection)


def solution(mesh):
    in_specs = (
        P(("batch", "mp"), None),
        P(("batch", "mp"), None),
        P(),
        P(("batch", "mp")),
        P(("batch", "mp")),
        P(("batch", "mp")),
    )
    out_specs = (P(("batch", "mp")), P(("batch", "mp"), None), P(("batch", "mp"), None), P())
    return jax.shard_map(
        per_device, mesh=mesh, in_specs=in_specs, out_specs=out_specs, check_vma=False
    )
```

```python
import jax
import jax.numpy as jnp
from jax import lax
from jax.experimental import pallas as pl
from jax.experimental.pallas import tpu as pltpu
from jax.sharding import PartitionSpec as P

inner_scale = 128.0
outer_scale = 8.0
loss_scale = 32.0
norm_eps = 1e-06
hidden_out = -1e30

NX, NZ, NYH, NMP = 4, 8, 4, 4
NG = NYH * NMP
NB = NX * NZ * NYH
MESH = pl.DeviceIdType.MESH
F32 = jnp.float32
BF16 = jnp.bfloat16
QN, QT, PN, PT = 8, 32, 10, 128
QR, PR, DIM, HID = QN * QT, PN * PT, 128, 768
TAIL = 16
HOPS = (1, 2, -1, -2)
CHUNK = 256


def exact_iota(shape, axis):
    return lax.broadcasted_iota(jnp.int32, shape, axis)


def nt_dot(left, right):
    return lax.dot_general(left, right, (((1,), (1,)), ((), ())), preferred_element_type=F32)


def log_sum(rows):
    top = jnp.maximum(jnp.maximum(rows[0], rows[1]), rows[2])
    return top + jnp.log(jnp.exp(rows[0] - top) + jnp.exp(rows[1] - top) + jnp.exp(rows[2] - top))


def step_kernel(
    qlen, plen, pos, qh_any, ph_any, proj_any,
    loss_out, ppre_out, qpre_out, total_out,
    qh, ph, proj, qbuf, qunit, qrad, paug, ptr, punit, prad, power, gsim,
    tops, tots, score, keeps, coef, member, lse_own, lse_in, tq_out, tq_in,
    ppre_t, ppart, src, r1, b2, b3, g4,
    in_sem, qs, qr, ls, lr, ts, tr, s1, q1, s2, q2, s3, q3, s4, q4,
):
    bi = lax.axis_index("batch")
    mi = lax.axis_index("mp")
    yh = bi % NYH
    z = (bi // NYH) % NZ
    x = bi // (NYH * NZ)
    g = yh * NMP + mi
    rows = HID // NG

    def ring_peer(hop):
        return ((bi + (hop + NB)) % NB, mi)

    def group_peer(o):
        j = (g + o) % NG
        return j, (bi - yh + j // NMP, j % NMP)

    def z_peer(o):
        j = (z + o) % NZ
        return j, (x * (NZ * NYH) + j * NYH + yh, mi)

    def x_peer(o):
        j = (x + o) % NX
        return j, (j * (NZ * NYH) + z * NYH + yh, mi)

    get_proj = pltpu.make_async_copy(proj_any, proj, in_sem.at[0])
    get_qh = pltpu.make_async_copy(qh_any, qh, in_sem.at[1])
    get_ph = pltpu.make_async_copy(ph_any, ph, in_sem.at[2])
    get_proj.start()
    get_qh.start()
    get_ph.start()

    barrier = pltpu.get_barrier_semaphore()
    for hop in HOPS:
        pl.semaphore_signal(barrier, inc=1, device_id=ring_peer(hop), device_id_type=MESH)
    for count, peer in ((NG, group_peer), (NZ, z_peer), (NX, x_peer)):
        @pl.loop(1, count)
        def _(o):
            pl.semaphore_signal(barrier, inc=1, device_id=peer(o)[1], device_id_type=MESH)

    lane = exact_iota((1, QR), 1)
    keep = jnp.zeros((1, QR), F32)
    for q in range(QN):
        token = lane - q * QT
        keep = jnp.where((token >= 0) & (token < qlen[q]), 1.0, keep)
    tail_row = exact_iota((TAIL, QR), 0)
    qbuf[0, DIM:DIM + TAIL, :] = jnp.where(
        tail_row == 0, 1.0, jnp.where(tail_row == 1, keep, 0.0)).astype(BF16)
    for b in range(3):
        qbuf[b, DIM + TAIL:, :] = jnp.zeros((QR - DIM - TAIL, QR), BF16)

    get_proj.wait()
    get_qh.wait()
    before = jnp.dot(qh[...], proj[...], preferred_element_type=F32).T
    radius = jnp.sqrt(jnp.sum(before * before, axis=0, keepdims=True) + norm_eps)
    unit = before / radius
    qunit[...] = unit
    qrad[...] = radius
    qbuf[0, :DIM, :] = unit.astype(BF16)

    pl.semaphore_wait(barrier, 4 + NG + NZ + NX - 3)

    def send_query(b):
        part = pl.ds(0, DIM + TAIL)
        return pltpu.make_async_remote_copy(
            src_ref=qbuf.at[0, part], dst_ref=qbuf.at[b, part], send_sem=qs.at[b - 1],
            recv_sem=qr.at[b - 1], device_id=ring_peer(b), device_id_type=MESH)

    send_query(1).start()
    send_query(2).start()

    member[...] = jnp.where(
        exact_iota((QR, QR), 0) // QT == exact_iota((QR, QR), 1) // QT, 1.0, 0.0)
    tops[...] = jnp.zeros(tops.shape, F32)
    tots[...] = jnp.ones(tots.shape, F32)

    @pl.loop(0, PN)
    def _(c):
        spot = pl.ds(pl.multiple_of(c * PT, PT), PT)
        outside = (exact_iota((PT, DIM), 0) >= plen[c]) & (exact_iota((PT, DIM), 1) == 0)
        paug[spot, DIM:] = jnp.where(outside, hidden_out, 0.0).astype(BF16)

    get_ph.wait()

    @pl.loop(0, PR // CHUNK)
    def _(r):
        spot = pl.ds(pl.multiple_of(r * CHUNK, CHUNK), CHUNK)
        before = jnp.dot(ph[spot, :], proj[...], preferred_element_type=F32)
        radius = jnp.sqrt(jnp.sum(before * before, axis=-1, keepdims=True) + norm_eps)
        unit = before / radius
        punit[spot, :] = unit
        prad[spot, :] = radius
        embed = unit.astype(BF16)
        paug[spot, :DIM] = embed * jnp.array(inner_scale, BF16)
        ptr[:, spot] = embed.astype(F32).T.astype(BF16)

    def forward(b):
        power[b] = jnp.dot(paug[...], qbuf[b], preferred_element_type=F32)

        @pl.loop(0, PN)
        def _(c):
            spot = pl.ds(pl.multiple_of(c * PT, PT), PT)
            logits = power[b, spot, :]
            top = jnp.max(logits, axis=0, keepdims=True)
            powers = jnp.exp(logits - top)
            power[b, spot, :] = powers
            tops[b, pl.ds(c, 1), :] = top
            tots[b, pl.ds(c, 1), :] = jnp.sum(powers, axis=0, keepdims=True)

        kept = qbuf[b, DIM:DIM + TAIL, :].astype(F32)[1:2, :]
        keeps[b] = jnp.broadcast_to(kept, (TAIL, QR))
        best = (jnp.log(tots[b]) + tops[b]) * (1.0 / inner_scale)
        scores = outer_scale * jnp.dot(
            best * kept, member[...], preferred_element_type=F32, precision=lax.Precision.HIGHEST)
        scores = jnp.where(exact_iota((TAIL, QR), 0) < PN, scores, hidden_out)
        score[b] = scores
        top = jnp.max(scores, axis=0, keepdims=True)
        total = top + jnp.log(jnp.sum(jnp.exp(scores - top), axis=0, keepdims=True))
        lse_own[pl.ds(b, 1), :] = total
        return total

    def to_grads(b, dscore):
        coef[...] = dscore * keeps[b] * (outer_scale * loss_scale) / tots[b]

        @pl.loop(0, PN)
        def _(c):
            spot = pl.ds(pl.multiple_of(c * PT, PT), PT)
            gsim[b, spot, :] = (power[b, spot, :] * coef[pl.ds(c, 1), :]).astype(BF16)

    def send_grad(b):
        return pltpu.make_async_remote_copy(
            src_ref=tq_out.at[b - 1], dst_ref=tq_in.at[b - 1], send_sem=ts.at[b - 1],
            recv_sem=tr.at[b - 1], device_id=ring_peer(-b), device_id_type=MESH)

    def send_lse(n):
        return pltpu.make_async_remote_copy(
            src_ref=lse_own, dst_ref=lse_in.at[n], send_sem=ls.at[n], recv_sem=lr.at[n],
            device_id=ring_peer(HOPS[n]), device_id_type=MESH)

    lse_own[...] = jnp.zeros(lse_own.shape, F32)
    forward(0)
    own = []
    for b in (1, 2):
        send_query(b).wait_recv()
        own.append(forward(b))
        if b == 2:
            for n in range(4):
                send_lse(n).start()
        to_grads(b, jnp.exp(score[b] - own[b - 1]))
        tq_out[b - 1] = jnp.dot(ptr[...], gsim[b], preferred_element_type=F32).astype(BF16)
        send_grad(b).start()

    for n in range(4):
        send_lse(n).wait_recv()
    totals = (
        log_sum((lse_own[0:1, :], lse_in[2, 1:2, :], lse_in[3, 2:3, :])),
        log_sum((lse_in[0, 0:1, :], lse_own[1:2, :], lse_in[2, 2:3, :])),
        log_sum((lse_in[1, 0:1, :], lse_in[0, 1:2, :], lse_own[2:3, :])),
    )
    place = jnp.zeros((1, QR), jnp.int32)
    for q in range(QN):
        place = jnp.where(lane // QT == q, pos[q], place)
    onehot = jnp.where(exact_iota((TAIL, QR), 0) == place, 1.0, 0.0)
    loss_out[...] = totals[0] - jnp.sum(onehot * score[0], axis=0, keepdims=True)
    for b in range(3):
        dscore = jnp.exp(score[b] - totals[b])
        to_grads(b, dscore - onehot if b == 0 else dscore)
    own_grad = jnp.dot(ptr[...], gsim[0], preferred_element_type=F32)
    qgrad = own_grad

    @pl.loop(0, PR // CHUNK)
    def _(r):
        spot = pl.ds(pl.multiple_of(r * CHUNK, CHUNK), CHUNK)
        grad = nt_dot(gsim[0, spot, :], qbuf[0, :DIM, :])
        grad += nt_dot(gsim[1, spot, :], qbuf[1, :DIM, :])
        grad += nt_dot(gsim[2, spot, :], qbuf[2, :DIM, :])
        unit = punit[spot, :]
        pre = (grad - unit * jnp.sum(unit * grad, axis=-1, keepdims=True)) / prad[spot, :]
        pre = pre.astype(BF16)
        ppre_out[spot, :] = pre
        ppre_t[:, spot] = pre.astype(F32).T.astype(BF16)

    ppart[...] = jnp.dot(ppre_t[...], ph[...], preferred_element_type=F32)

    send_grad(1).wait_recv()
    send_grad(2).wait_recv()
    qgrad += jnp.exp(lse_in[2, 1:2, :] - totals[0]) * tq_in[0].astype(F32)
    qgrad += jnp.exp(lse_in[3, 2:3, :] - totals[0]) * tq_in[1].astype(F32)
    unit = qunit[...]
    pre = (qgrad - unit * jnp.sum(unit * qgrad, axis=0, keepdims=True)) / qrad[...]
    pre = pre.astype(BF16)
    qpre_out[...] = pre
    part = ppart[...] + jnp.dot(pre, qh[...], preferred_element_type=F32)
    for t in range(HID // DIM):
        src[t * DIM:(t + 1) * DIM, :] = part[:, t * DIM:(t + 1) * DIM].astype(BF16)

    def piece(j):
        return pl.ds(pl.multiple_of(j * rows, rows), rows)

    def exchange(count, peer, source, target, mine, send, recv):
        def copy(o):
            j, where = peer(o)
            return pltpu.make_async_remote_copy(
                src_ref=source(j), dst_ref=target(mine), send_sem=send.at[o],
                recv_sem=recv.at[mine], device_id=where, device_id_type=MESH)

        def arrival(o):
            j, where = peer(o)
            return pltpu.make_async_remote_copy(
                src_ref=source(j), dst_ref=target(j), send_sem=send.at[o], recv_sem=recv.at[j],
                device_id=where, device_id_type=MESH)

        @pl.loop(1, count)
        def _(o):
            copy(o).start()

        @pl.loop(1, count)
        def _(o):
            arrival(o).wait_recv()

        def finish():
            @pl.loop(1, count)
            def _(o):
                copy(o).wait_send()

        return finish

    r1[g] = src[piece(g), :]
    done1 = exchange(
        NG, group_peer, lambda j: src.at[piece(j)], lambda j: r1.at[j], g, s1, q1)
    b2[z] = jnp.sum(r1[...].astype(F32), axis=0).astype(BF16)
    done2 = exchange(NZ, z_peer, lambda j: b2.at[z], lambda j: b2.at[j], z, s2, q2)
    b3[x] = jnp.sum(b2[...].astype(F32), axis=0).astype(BF16)
    done3 = exchange(NX, x_peer, lambda j: b3.at[x], lambda j: b3.at[j], x, s3, q3)
    g4[piece(g), :] = jnp.sum(b3[...].astype(F32), axis=0).astype(BF16)
    done4 = exchange(
        NG, group_peer, lambda j: g4.at[piece(g)], lambda j: g4.at[piece(j)], g, s4, q4)
    total_out[...] = g4[...]
    for done in (done1, done2, done3, done4):
        done()
    for b in (1, 2):
        send_query(b).wait_send()
        send_grad(b).wait_send()
    for n in range(4):
        send_lse(n).wait_send()


def run_step(query_lengths, passage_lengths, positives, query_hidden, passage_hidden, projection):
    dma = pltpu.SemaphoreType.DMA
    smem = pl.BlockSpec(memory_space=pltpu.SMEM)
    vmem = pl.BlockSpec(memory_space=pltpu.VMEM)
    hbm = pl.BlockSpec(memory_space=pl.ANY)
    part = HID // NG
    vm = pltpu.VMEM
    return pl.pallas_call(
        step_kernel,
        out_shape=(
            jax.ShapeDtypeStruct((1, QR), F32),
            jax.ShapeDtypeStruct((PR, DIM), BF16),
            jax.ShapeDtypeStruct((DIM, QR), BF16),
            jax.ShapeDtypeStruct((HID, DIM), BF16),
        ),
        in_specs=[smem, smem, smem, hbm, hbm, hbm],
        out_specs=(vmem, vmem, vmem, vmem),
        scratch_shapes=[
            vm((QR, HID), BF16), vm((PR, HID), BF16), vm((HID, DIM), BF16),
            vm((3, QR, QR), BF16), vm((DIM, QR), F32), vm((1, QR), F32),
            vm((PR, 2 * DIM), BF16), vm((DIM, PR), BF16), vm((PR, DIM), F32), vm((PR, 1), F32),
            vm((3, PR, QR), F32), vm((3, PR, QR), BF16),
            vm((3, TAIL, QR), F32), vm((3, TAIL, QR), F32), vm((3, TAIL, QR), F32),
            vm((3, TAIL, QR), F32), vm((TAIL, QR), F32), vm((QR, QR), F32),
            vm((8, QR), F32), vm((4, 8, QR), F32),
            vm((2, DIM, QR), BF16), vm((2, DIM, QR), BF16),
            vm((DIM, PR), BF16), vm((DIM, HID), F32),
            vm((HID, DIM), BF16), vm((NG, part, DIM), BF16), vm((NZ, part, DIM), BF16),
            vm((NX, part, DIM), BF16), vm((HID, DIM), BF16),
            dma((3,)), dma((2,)), dma((2,)), dma((4,)), dma((4,)), dma((2,)), dma((2,)),
            dma((NG,)), dma((NG,)), dma((NZ,)), dma((NZ,)), dma((NX,)), dma((NX,)), dma((NG,)), dma((NG,)),
        ],
        compiler_params=pltpu.CompilerParams(collective_id=0, has_side_effects=True),
    )(query_lengths, passage_lengths, positives, query_hidden, passage_hidden, projection)


def finish_kernel(loss, ppre, qpre, proj, total, loss_out, gq_any, gp_any, gproj, held, sem):
    for q in range(QN):
        loss_out[q] = loss[0, q * QT]

    def copy(r):
        spot = pl.ds(r * CHUNK, CHUNK)
        where = gq_any if r == PR // CHUNK else gp_any.at[spot]
        return pltpu.make_async_copy(held.at[spot], where, sem.at[r])

    for r in range(PR // CHUNK + 1):
        spot = pl.ds(r * CHUNK, CHUNK)
        if r == PR // CHUNK:
            pre = qpre[...].astype(F32).T.astype(BF16)
        else:
            pre = ppre[spot, :]
        held[spot, :] = nt_dot(pre, proj[...]).astype(BF16)
        copy(r).start()
    for t in range(HID // DIM):
        spot = pl.ds(t * DIM, DIM)
        gproj[spot, :] = total[spot, :].astype(F32).T * (1.0 / (NB * NMP))
    for r in range(PR // CHUNK + 1):
        copy(r).wait()


def run_finish(loss, ppre, qpre, projection, total):
    smem = pl.BlockSpec(memory_space=pltpu.SMEM)
    vmem = pl.BlockSpec(memory_space=pltpu.VMEM)
    hbm = pl.BlockSpec(memory_space=pl.ANY)
    return pl.pallas_call(
        finish_kernel,
        out_shape=(
            jax.ShapeDtypeStruct((QN,), F32),
            jax.ShapeDtypeStruct((QR, HID), BF16),
            jax.ShapeDtypeStruct((PR, HID), BF16),
            jax.ShapeDtypeStruct((HID, DIM), F32),
        ),
        in_specs=[smem, vmem, vmem, vmem, vmem],
        out_specs=(smem, hbm, hbm, vmem),
        scratch_shapes=[
            pltpu.VMEM((PR + QR, HID), BF16),
            pltpu.SemaphoreType.DMA((PR // CHUNK + 1,)),
        ],
    )(loss, ppre, qpre, projection, total)


def per_device(query_hidden, passage_hidden, projection, query_lengths, passage_lengths, positives):
    loss, ppre, qpre, total = run_step(
        query_lengths, passage_lengths, positives, query_hidden, passage_hidden, projection)
    return run_finish(loss, ppre, qpre, projection, total)


def solution(mesh):
    in_specs = (
        P(("batch", "mp"), None),
        P(("batch", "mp"), None),
        P(),
        P(("batch", "mp")),
        P(("batch", "mp")),
        P(("batch", "mp")),
    )
    out_specs = (P(("batch", "mp")), P(("batch", "mp"), None), P(("batch", "mp"), None), P())
    return jax.shard_map(
        per_device, mesh=mesh, in_specs=in_specs, out_specs=out_specs, check_vma=False
    )
```

```python
import jax
import jax.numpy as jnp
from jax import lax
from jax.experimental import pallas as pl
from jax.experimental.pallas import tpu as pltpu
from jax.sharding import PartitionSpec as P

inner_scale = 128.0
outer_scale = 8.0
loss_scale = 32.0
norm_eps = 1e-06
hidden_out = -1e30

NX, NZ, NYH, NYL, NC = 4, 8, 4, 2, 2
NMP = NYL * NC
NB = NX * NZ * NYH
MESH = pl.DeviceIdType.MESH
F32 = jnp.float32
BF16 = jnp.bfloat16
QN, QT, PN, PT = 8, 32, 10, 128
QR, PR, DIM, HID = QN * QT, PN * PT, 128, 768
TAIL = 16
HOPS = (1, 2, -1, -2)
CHUNK = 256
UNROLL = 2


def exact_iota(shape, axis):
    return lax.broadcasted_iota(jnp.int32, shape, axis)


def nt_dot(left, right):
    return lax.dot_general(left, right, (((1,), (1,)), ((), ())), preferred_element_type=F32)


def log_sum(rows):
    top = jnp.maximum(jnp.maximum(rows[0], rows[1]), rows[2])
    return top + jnp.log(jnp.exp(rows[0] - top) + jnp.exp(rows[1] - top) + jnp.exp(rows[2] - top))


def turned(here, count):
    order = sorted(range(count), key=lambda a: -min(a, count - a))
    spots = []
    for a in order:
        there = here + a
        spots.append((a, jnp.where(there >= count, there - count, there) if a else here))
    return spots


def step_kernel(
    qlen, plen, pos, qh_any, ph_any, proj_any,
    loss_out, ppre_any, qpre_any, total_out,
    qh, ph, proj, qbuf, qunit, qrad, paug, ptr, punit, prad, power, gsim,
    tops, tots, score, keeps, coef, member, lse_own, lse_in, tq_out, tq_in, qscaled,
    ppre, ppre_t, qpre, ppart, src, a1, a2, a3, b1, b2, b3, c1, c2, c3, gathered,
    in_sem, out_sem, qs, qr, ls, lr, ts, tr, push, pull,
):
    bi = lax.axis_index("batch")
    mi = lax.axis_index("mp")
    yh = lax.rem(bi, NYH)
    up = lax.div(bi, NYH)
    z = lax.rem(up, NZ)
    x = lax.div(up, NZ)
    yl = lax.div(mi, NC)
    core = lax.rem(mi, NC)
    y = yh * NYL + yl
    xz = bi - yh
    cores = turned(core, NC)

    def at_y(spot, side):
        return (xz + lax.div(spot, NYL), lax.rem(spot, NYL) * NC + side)

    def at_z(spot, side):
        return (bi + (spot - z) * NYH, mi + (side - core))

    def at_x(spot, side):
        return (bi + (spot - x) * (NYH * NZ), mi + (side - core))

    def pairs(spots, place):
        return [(spot * NC + side, place(spot, side)) for a, spot in spots for c, side in cores if a or c]

    def lines(spots, place):
        return [(spot, place(spot, core)) for a, spot in spots if a]

    ys, zs, xs = turned(y, NYH * NYL), turned(z, NZ), turned(x, NX)
    y_pairs, z_pairs, x_pairs = pairs(ys, at_y), pairs(zs, at_z), pairs(xs, at_x)
    y_line, z_line, x_line = lines(ys, at_y), lines(zs, at_z), lines(xs, at_x)

    def ring_peer(hop):
        there = bi + hop
        there = jnp.where(there >= NB, there - NB, there) if hop > 0 else jnp.where(there < 0, there + NB, there)
        return (there, mi)

    ring = {hop: ring_peer(hop) for hop in HOPS}

    get_proj = pltpu.make_async_copy(proj_any, proj, in_sem.at[0])
    get_qh = pltpu.make_async_copy(qh_any, qh, in_sem.at[1])
    get_ph = pltpu.make_async_copy(ph_any, ph, in_sem.at[2])
    get_proj.start()
    get_qh.start()
    get_ph.start()

    barrier = pltpu.get_barrier_semaphore()
    everyone = [ring[hop] for hop in HOPS] + [w for _, w in y_pairs + z_pairs + x_pairs]
    for where in everyone:
        pl.semaphore_signal(barrier, inc=1, device_id=where, device_id_type=MESH)

    lane = exact_iota((1, QR), 1)
    keep = jnp.zeros((1, QR), F32)
    for q in range(QN):
        token = lane - q * QT
        keep = jnp.where((token >= 0) & (token < qlen[q]), 1.0, keep)
    tail_row = exact_iota((TAIL, QR), 0)
    qbuf[0, DIM:DIM + TAIL, :] = jnp.where(
        tail_row == 0, 1.0, jnp.where(tail_row == 1, keep, 0.0)).astype(BF16)
    for b in range(3):
        qbuf[b, DIM + TAIL:, :] = jnp.zeros((QR - DIM - TAIL, QR), BF16)

    get_proj.wait()
    get_qh.wait()
    before = jnp.dot(qh[...], proj[...], preferred_element_type=F32).T
    radius = jnp.sqrt(jnp.sum(before * before, axis=0, keepdims=True) + norm_eps)
    inverse = 1.0 / radius
    unit = before * inverse
    qunit[...] = unit
    qrad[...] = inverse
    qbuf[0, :DIM, :] = unit.astype(BF16)

    pl.semaphore_wait(barrier, len(everyone))

    def send_query(b):
        part = pl.ds(0, DIM + TAIL)
        return pltpu.make_async_remote_copy(
            src_ref=qbuf.at[0, part], dst_ref=qbuf.at[b, part], send_sem=qs.at[b - 1],
            recv_sem=qr.at[b - 1], device_id=ring[b], device_id_type=MESH)

    send_query(2).start()
    send_query(1).start()

    member[...] = jnp.where(
        exact_iota((QR, QR), 0) // QT == exact_iota((QR, QR), 1) // QT, 1.0, 0.0).astype(BF16)
    tops[...] = jnp.zeros(tops.shape, F32)
    tots[...] = jnp.ones(tots.shape, F32)

    @pl.loop(0, PN)
    def _(c):
        spot = pl.ds(pl.multiple_of(c * PT, PT), PT)
        outside = (exact_iota((PT, DIM), 0) >= plen[c]) & (exact_iota((PT, DIM), 1) == 0)
        paug[spot, DIM:] = jnp.where(outside, hidden_out, 0.0).astype(BF16)

    get_ph.wait()

    for r in range(PR // CHUNK):
        spot = pl.ds(r * CHUNK, CHUNK)
        before = jnp.dot(ph[spot, :], proj[...], preferred_element_type=F32)
        radius = jnp.sqrt(jnp.sum(before * before, axis=-1, keepdims=True) + norm_eps)
        inverse = 1.0 / radius
        unit = before * inverse
        punit[spot, :] = unit
        prad[spot, :] = inverse
        embed = unit.astype(BF16)
        paug[spot, :DIM] = embed * jnp.array(inner_scale, BF16)
        ptr[:, spot] = embed.astype(F32).T.astype(BF16)

    def forward(b):
        power[b] = jnp.dot(paug[...], qbuf[b], preferred_element_type=F32)

        @pl.loop(0, PN // UNROLL)
        def _(step):
            for k in range(UNROLL):
                c = step * UNROLL + k
                spot = pl.ds(pl.multiple_of(c * PT, PT), PT)
                logits = power[b, spot, :]
                top = jnp.max(logits, axis=0, keepdims=True)
                powers = jnp.exp(logits - top)
                power[b, spot, :] = powers
                tops[b, pl.ds(c, 1), :] = top
                tots[b, pl.ds(c, 1), :] = jnp.sum(powers, axis=0, keepdims=True)

        kept = qbuf[b, DIM:DIM + TAIL, :].astype(F32)[1:2, :]
        keeps[b] = jnp.broadcast_to(kept, (TAIL, QR))
        best = (jnp.log(tots[b]) + tops[b]) * (1.0 / inner_scale) * kept
        high = best.astype(BF16)
        rest = best - high.astype(F32)
        middle = rest.astype(BF16)
        low = (rest - middle.astype(F32)).astype(BF16)
        sums = jnp.dot(
            jnp.concatenate([high, middle, low], axis=0), member[...], preferred_element_type=F32)
        scores = outer_scale * (sums[:TAIL] + (sums[TAIL:2 * TAIL] + sums[2 * TAIL:]))
        scores = jnp.where(exact_iota((TAIL, QR), 0) < PN, scores, hidden_out)
        score[b] = scores
        top = jnp.max(scores, axis=0, keepdims=True)
        total = top + jnp.log(jnp.sum(jnp.exp(scores - top), axis=0, keepdims=True))
        lse_own[pl.ds(b, 1), :] = total
        return total

    def to_grads(b, dscore):
        coef[...] = dscore * keeps[b] * (outer_scale * loss_scale) / tots[b]

        @pl.loop(0, PN // UNROLL)
        def _(step):
            for k in range(UNROLL):
                c = step * UNROLL + k
                spot = pl.ds(pl.multiple_of(c * PT, PT), PT)
                gsim[b, spot, :] = (power[b, spot, :] * coef[pl.ds(c, 1), :]).astype(BF16)

    def send_grad(b):
        return pltpu.make_async_remote_copy(
            src_ref=tq_out.at[b - 1], dst_ref=tq_in.at[b - 1], send_sem=ts.at[b - 1],
            recv_sem=tr.at[b - 1], device_id=ring[-b], device_id_type=MESH)

    def send_lse(n):
        return pltpu.make_async_remote_copy(
            src_ref=lse_own, dst_ref=lse_in.at[n], send_sem=ls.at[n], recv_sem=lr.at[n],
            device_id=ring[HOPS[n]], device_id_type=MESH)

    lse_own[...] = jnp.zeros(lse_own.shape, F32)
    own = [forward(0)]
    for b in (1, 2):
        send_query(b).wait_recv()
        own.append(forward(b))
    for n in range(4):
        send_lse(n).start()
    for b in (2, 1):
        to_grads(b, jnp.exp(score[b] - lse_own[b:b + 1, :]))
        tq_out[b - 1] = jnp.dot(ptr[...], gsim[b], preferred_element_type=F32).astype(BF16)
        send_grad(b).start()

    place = jnp.zeros((1, QR), jnp.int32)
    for q in range(QN):
        place = jnp.where(lane // QT == q, pos[q], place)
    onehot = jnp.where(exact_iota((TAIL, QR), 0) == place, 1.0, 0.0)

    for n in range(4):
        send_lse(n).wait_recv()
    totals = (
        log_sum((lse_own[0:1, :], lse_in[2, 1:2, :], lse_in[3, 2:3, :])),
        log_sum((lse_in[0, 0:1, :], lse_own[1:2, :], lse_in[2, 2:3, :])),
        log_sum((lse_in[1, 0:1, :], lse_in[0, 1:2, :], lse_own[2:3, :])),
    )
    loss_out[...] = totals[0] - jnp.sum(onehot * score[0], axis=0, keepdims=True)
    for b in (1, 2):
        factor = jnp.exp(lse_own[b:b + 1, :] - totals[b])
        qscaled[b - 1] = (qbuf[b, :DIM, :].astype(F32) * factor).astype(BF16)
    to_grads(0, jnp.exp(score[0] - totals[0]) - onehot)

    for r in range(PR // CHUNK):
        spot = pl.ds(r * CHUNK, CHUNK)
        grad = nt_dot(gsim[0, spot, :], qbuf[0, :DIM, :])
        grad += nt_dot(gsim[1, spot, :], qscaled[0])
        grad += nt_dot(gsim[2, spot, :], qscaled[1])
        unit = punit[spot, :]
        pre = (grad - unit * jnp.sum(unit * grad, axis=-1, keepdims=True)) * prad[spot, :]
        pre = pre.astype(BF16)
        ppre[spot, :] = pre
        ppre_t[:, spot] = pre.astype(F32).T.astype(BF16)

    put_ppre = pltpu.make_async_copy(ppre, ppre_any, out_sem.at[0])
    put_ppre.start()
    ppart[...] = jnp.dot(ppre_t[...], ph[...], preferred_element_type=F32)
    qgrad = jnp.dot(ptr[...], gsim[0], preferred_element_type=F32)

    send_grad(1).wait_recv()
    send_grad(2).wait_recv()
    qgrad += jnp.exp(lse_in[2, 1:2, :] - totals[0]) * tq_in[0].astype(F32)
    qgrad += jnp.exp(lse_in[3, 2:3, :] - totals[0]) * tq_in[1].astype(F32)
    unit = qunit[...]
    pre = (qgrad - unit * jnp.sum(unit * qgrad, axis=0, keepdims=True)) * qrad[...]
    pre = pre.astype(BF16)
    qpre[...] = pre
    part = ppart[...] + jnp.dot(pre, qh[...], preferred_element_type=F32)
    for t in range(HID // DIM):
        src[t * DIM:(t + 1) * DIM, :] = part[:, t * DIM:(t + 1) * DIM].astype(BF16)
    put_qpre = pltpu.make_async_copy(qpre, qpre_any, out_sem.at[1])

    def piece(first, size, j):
        return pl.ds(pl.multiple_of(first + j * size, size), size)

    def start(stage, peers, source, target, mine):
        for j, where in peers:
            pltpu.make_async_remote_copy(
                src_ref=source(j), dst_ref=target(mine), send_sem=push.at[stage],
                recv_sem=pull.at[stage], device_id=where, device_id_type=MESH).start()

    def bulk(stage, peers, whole):
        return pltpu.make_async_remote_copy(
            src_ref=whole, dst_ref=whole, send_sem=push.at[stage], recv_sem=pull.at[stage],
            device_id=peers[0][1], device_id_type=MESH)

    def added(box):
        return jnp.sum(box[...].astype(F32), axis=0).astype(BF16)

    plan = []
    first = 0
    for boxes, group, mine, then in (
        ((c1, c2, c3), x_pairs, x * NC + core, ((y_line, y), (z_line, z))),
        ((a1, a2, a3), y_pairs, y * NC + core, ((z_line, z), (x_line, x))),
        ((b1, b2, b3), z_pairs, z * NC + core, ((y_line, y), (x_line, x))),
    ):
        plan.append((first, boxes, group, mine, then))
        first += boxes[0].shape[0] * boxes[0].shape[1]

    def whole_of(box, peers):
        return box.at[pl.ds(0, len(peers))]

    for n, (first, boxes, group, mine, then) in enumerate(plan):
        size = boxes[0].shape[1]
        start(4 * n, group, lambda j: src.at[piece(first, size, j)], lambda j: boxes[0].at[j], mine)
        boxes[0][mine] = src[piece(first, size, mine), :]
    put_qpre.start()
    for hop in range(2):
        for n, (first, boxes, group, mine, then) in enumerate(plan):
            peers, here = then[hop]
            came = group if hop == 0 else then[0][0]
            bulk(4 * n + hop, came, whole_of(boxes[hop], came)).wait_recv()
            box = boxes[hop + 1]
            box[here] = added(boxes[hop])
            start(4 * n + 1 + hop, peers, lambda j: box.at[here], lambda j: box.at[j], here)
    for n, (first, boxes, group, mine, then) in enumerate(plan):
        size = boxes[0].shape[1]
        bulk(4 * n + 2, then[1][0], whole_of(boxes[2], then[1][0])).wait_recv()
        gathered[piece(first, size, mine), :] = added(boxes[2])
        start(
            4 * n + 3, group, lambda j: gathered.at[piece(first, size, mine)],
            lambda j: gathered.at[piece(first, size, j)], mine)
    for n, (first, boxes, group, mine, then) in enumerate(plan):
        size = boxes[0].shape[1]
        whole = gathered.at[pl.ds(first, len(group) * size)]
        bulk(4 * n + 3, group, whole).wait_recv()
    total_out[...] = gathered[...]

    for n, (first, boxes, group, mine, then) in enumerate(plan):
        size = boxes[0].shape[1]
        bulk(4 * n, group, whole_of(boxes[0], group)).wait_send()
        for hop in range(2):
            bulk(4 * n + 1 + hop, then[hop][0], whole_of(boxes[hop + 1], then[hop][0])).wait_send()
        bulk(4 * n + 3, group, gathered.at[pl.ds(first, len(group) * size)]).wait_send()
    for b in (1, 2):
        send_query(b).wait_send()
        send_grad(b).wait_send()
    for n in range(4):
        send_lse(n).wait_send()
    put_ppre.wait()
    put_qpre.wait()


def run_step(query_lengths, passage_lengths, positives, query_hidden, passage_hidden, projection):
    dma = pltpu.SemaphoreType.DMA
    smem = pl.BlockSpec(memory_space=pltpu.SMEM)
    vmem = pl.BlockSpec(memory_space=pltpu.VMEM)
    hbm = pl.BlockSpec(memory_space=pl.ANY)
    vm = pltpu.VMEM
    ny = NYH * NYL
    share = HID // 3
    ya, za, xa = ny * NC, NZ * NC, NX * NC
    return pl.pallas_call(
        step_kernel,
        out_shape=(
            jax.ShapeDtypeStruct((1, QR), F32),
            jax.ShapeDtypeStruct((PR, DIM), BF16),
            jax.ShapeDtypeStruct((DIM, QR), BF16),
            jax.ShapeDtypeStruct((HID, DIM), BF16),
        ),
        in_specs=[smem, smem, smem, hbm, hbm, hbm],
        out_specs=(vmem, hbm, hbm, vmem),
        scratch_shapes=[
            vm((QR, HID), BF16), vm((PR, HID), BF16), vm((HID, DIM), BF16),
            vm((3, QR, QR), BF16), vm((DIM, QR), F32), vm((1, QR), F32),
            vm((PR, 2 * DIM), BF16), vm((DIM, PR), BF16), vm((PR, DIM), F32), vm((PR, 1), F32),
            vm((3, PR, QR), F32), vm((3, PR, QR), BF16),
            vm((3, TAIL, QR), F32), vm((3, TAIL, QR), F32), vm((3, TAIL, QR), F32),
            vm((3, TAIL, QR), F32), vm((TAIL, QR), F32), vm((QR, QR), BF16),
            vm((8, QR), F32), vm((4, 8, QR), F32),
            vm((2, DIM, QR), BF16), vm((2, DIM, QR), BF16), vm((2, DIM, QR), BF16),
            vm((PR, DIM), BF16), vm((DIM, PR), BF16), vm((DIM, QR), BF16), vm((DIM, HID), F32),
            vm((HID, DIM), BF16),
            vm((ya, share // ya, DIM), BF16), vm((NZ, share // ya, DIM), BF16), vm((NX, share // ya, DIM), BF16),
            vm((za, share // za, DIM), BF16), vm((ny, share // za, DIM), BF16), vm((NX, share // za, DIM), BF16),
            vm((xa, share // xa, DIM), BF16), vm((ny, share // xa, DIM), BF16), vm((NZ, share // xa, DIM), BF16),
            vm((HID, DIM), BF16),
            dma((3,)), dma((2,)), dma((2,)), dma((2,)), dma((4,)), dma((4,)), dma((2,)), dma((2,)),
            dma((12,)), dma((12,)),
        ],
        compiler_params=pltpu.CompilerParams(collective_id=0, has_side_effects=True),
    )(query_lengths, passage_lengths, positives, query_hidden, passage_hidden, projection)


def finish_kernel(loss, ppre, qpre, proj, total, loss_out, gq_any, gp_any, gproj, held, sem):
    for q in range(QN):
        loss_out[q] = loss[0, q * QT]
    copies = []
    for t in range(HID // QR):
        columns = pl.ds(t * QR, QR)
        for h in range(2):
            spot = pl.ds(h * (PR // 2), PR // 2)
            held[spot, columns] = nt_dot(ppre[spot, :], proj[columns, :]).astype(BF16)
            copies.append(pltpu.make_async_copy(
                held.at[spot, columns], gp_any.at[spot, columns], sem.at[len(copies)]))
            copies[-1].start()
        if t == 0:
            spot = pl.ds(PR, QR)
            pre = qpre[...].astype(F32).T.astype(BF16)
            held[spot, :] = nt_dot(pre, proj[...]).astype(BF16)
            copies.append(pltpu.make_async_copy(held.at[spot], gq_any, sem.at[len(copies)]))
            copies[-1].start()
            for n in range(HID // DIM):
                spot = pl.ds(n * DIM, DIM)
                gproj[spot, :] = total[spot, :].astype(F32).T * (1.0 / (NB * NMP))
    for copy in copies:
        copy.wait()


def run_finish(loss, ppre, qpre, projection, total):
    smem = pl.BlockSpec(memory_space=pltpu.SMEM)
    vmem = pl.BlockSpec(memory_space=pltpu.VMEM)
    hbm = pl.BlockSpec(memory_space=pl.ANY)
    return pl.pallas_call(
        finish_kernel,
        out_shape=(
            jax.ShapeDtypeStruct((QN,), F32),
            jax.ShapeDtypeStruct((QR, HID), BF16),
            jax.ShapeDtypeStruct((PR, HID), BF16),
            jax.ShapeDtypeStruct((HID, DIM), F32),
        ),
        in_specs=[smem, vmem, vmem, vmem, vmem],
        out_specs=(smem, hbm, hbm, vmem),
        scratch_shapes=[
            pltpu.VMEM((PR + QR, HID), BF16),
            pltpu.SemaphoreType.DMA((2 * (HID // QR) + 1,)),
        ],
    )(loss, ppre, qpre, projection, total)


def per_device(query_hidden, passage_hidden, projection, query_lengths, passage_lengths, positives):
    loss, ppre, qpre, total = run_step(
        query_lengths, passage_lengths, positives, query_hidden, passage_hidden, projection)
    return run_finish(loss, ppre, qpre, projection, total)


def solution(mesh):
    in_specs = (
        P(("batch", "mp"), None),
        P(("batch", "mp"), None),
        P(),
        P(("batch", "mp")),
        P(("batch", "mp")),
        P(("batch", "mp")),
    )
    out_specs = (P(("batch", "mp")), P(("batch", "mp"), None), P(("batch", "mp"), None), P())
    return jax.shard_map(
        per_device, mesh=mesh, in_specs=in_specs, out_specs=out_specs, check_vma=False
    )
```

```python
import jax
import jax.numpy as jnp
from jax import lax
from jax.experimental import pallas as pl
from jax.experimental.pallas import tpu as pltpu
from jax.sharding import PartitionSpec as P

inner_scale = 128.0
outer_scale = 8.0
loss_scale = 32.0
norm_eps = 1e-06
hidden_out = -1e30

NX, NZ, NYH, NYL, NC = 4, 8, 4, 2, 2
NMP = NYL * NC
NB = NX * NZ * NYH
MESH = pl.DeviceIdType.MESH
F32 = jnp.float32
BF16 = jnp.bfloat16
QN, QT, PN, PT = 8, 32, 10, 128
QR, PR, DIM, HID = QN * QT, PN * PT, 128, 768
TAIL = 16
HOPS = (1, 2, -1, -2)
CHUNK = 256
UNROLL = 2


def exact_iota(shape, axis):
    return lax.broadcasted_iota(jnp.int32, shape, axis)


def nt_dot(left, right):
    return lax.dot_general(left, right, (((1,), (1,)), ((), ())), preferred_element_type=F32)


def log_sum(rows):
    top = jnp.maximum(jnp.maximum(rows[0], rows[1]), rows[2])
    return top + jnp.log(jnp.exp(rows[0] - top) + jnp.exp(rows[1] - top) + jnp.exp(rows[2] - top))


def turned(here, count):
    order = sorted(range(count), key=lambda a: -min(a, count - a))
    spots = []
    for a in order:
        there = here + a
        spots.append((a, jnp.where(there >= count, there - count, there) if a else here))
    return spots


def step_kernel(
    qlen_any, plen_any, pos_any, qh_any, ph_any, proj_any,
    loss_out, hidden_out_ref, total_out,
    qlen, plen, pos, both, proj, qbuf, qunit, qrad, paug, ptr, punit, prad, power, gsim,
    tops, tots, score, keeps, coef, member, lse_own, lse_in, tq_out, tq_in, qscaled,
    ppre, pre_t, src, a1, a2, a3, a4, b1, b2, b3, b4, c1, c2, c3, c4, gathered,
    in_sem, qs, qr, ls, lr, ts, tr, push, pull,
):
    bi = lax.axis_index("batch")
    mi = lax.axis_index("mp")
    yh = lax.rem(bi, NYH)
    up = lax.div(bi, NYH)
    z = lax.rem(up, NZ)
    x = lax.div(up, NZ)
    yl = lax.div(mi, NC)
    core = lax.rem(mi, NC)
    y = yh * NYL + yl
    xz = bi - yh

    def at_y(spot):
        return (xz + lax.div(spot, NYL), lax.rem(spot, NYL) * NC + core)

    def at_z(spot):
        return (bi + (spot - z) * NYH, mi)

    def at_x(spot):
        return (bi + (spot - x) * (NYH * NZ), mi)

    def line(here, count, place):
        return [(spot, place(spot)) for a, spot in turned(here, count) if a]

    def ring_peer(hop):
        there = bi + hop
        there = jnp.where(there >= NB, there - NB, there) if hop > 0 else jnp.where(there < 0, there + NB, there)
        return (there, mi)

    ring = {hop: ring_peer(hop) for hop in HOPS}

    whole_p, whole_q = pl.ds(0, PR), pl.ds(PR, QR)
    get_proj = pltpu.make_async_copy(proj_any, proj, in_sem.at[0])
    get_qh = pltpu.make_async_copy(qh_any, both.at[whole_q], in_sem.at[1])
    get_ph = pltpu.make_async_copy(ph_any, both.at[whole_p], in_sem.at[2])

    small = [
        pltpu.make_async_copy(far, near, in_sem.at[3 + n])
        for n, (far, near) in enumerate(((qlen_any, qlen), (plen_any, plen), (pos_any, pos)))]

    @pl.when(bi >= 0)
    def _():
        for copy in small:
            copy.start()
        get_proj.start()
        get_qh.start()
        get_ph.start()

    barrier = pltpu.get_barrier_semaphore()

    def greet(places):
        for where in places:
            pl.semaphore_signal(barrier, inc=1, device_id=where, device_id_type=MESH)
        return len(places)

    greeted = greet([ring[hop] for hop in HOPS])
    y_line = line(y, NYH * NYL, at_y)
    z_line = line(z, NZ, at_z)
    x_line = line(x, NX, at_x)
    partner = [(NC - 1 - core, (bi, mi + (NC - 1 - 2 * core)))]
    greeted += greet([where for _, where in y_line + z_line + x_line + partner])

    for copy in small:
        copy.wait()
    lane = exact_iota((1, QR), 1)
    keep = jnp.zeros((1, QR), F32)
    for q in range(QN):
        token = lane - q * QT
        keep = jnp.where((token >= 0) & (token < qlen[q]), 1.0, keep)
    tail_row = exact_iota((TAIL, QR), 0)
    qbuf[0, DIM:DIM + TAIL, :] = jnp.where(
        tail_row == 0, 1.0, jnp.where(tail_row == 1, keep, 0.0)).astype(BF16)
    for b in range(3):
        qbuf[b, DIM + TAIL:, :] = jnp.zeros((QR - DIM - TAIL, QR), BF16)

    get_proj.wait()
    get_qh.wait()
    before = jnp.dot(both[whole_q, :], proj[...], preferred_element_type=F32).T
    radius = jnp.sqrt(jnp.sum(before * before, axis=0, keepdims=True) + norm_eps)
    inverse = 1.0 / radius
    unit = before * inverse
    qunit[...] = unit
    qrad[...] = inverse
    qbuf[0, :DIM, :] = unit.astype(BF16)

    pl.semaphore_wait(barrier, greeted)

    def send_query(b):
        part = pl.ds(0, DIM + TAIL)
        return pltpu.make_async_remote_copy(
            src_ref=qbuf.at[0, part], dst_ref=qbuf.at[b, part], send_sem=qs.at[b - 1],
            recv_sem=qr.at[b - 1], device_id=ring[b], device_id_type=MESH)

    send_query(2).start()
    send_query(1).start()

    member[...] = jnp.where(
        exact_iota((QR, QR), 0) // QT == exact_iota((QR, QR), 1) // QT, 1.0, 0.0).astype(BF16)
    tops[...] = jnp.zeros(tops.shape, F32)
    tots[...] = jnp.ones(tots.shape, F32)

    @pl.loop(0, PN)
    def _(c):
        spot = pl.ds(pl.multiple_of(c * PT, PT), PT)
        outside = (exact_iota((PT, DIM), 0) >= plen[c]) & (exact_iota((PT, DIM), 1) == 0)
        paug[spot, DIM:] = jnp.where(outside, hidden_out, 0.0).astype(BF16)

    get_ph.wait()

    for r in range(PR // CHUNK):
        spot = pl.ds(r * CHUNK, CHUNK)
        before = jnp.dot(both[spot, :], proj[...], preferred_element_type=F32)
        radius = jnp.sqrt(jnp.sum(before * before, axis=-1, keepdims=True) + norm_eps)
        inverse = 1.0 / radius
        unit = before * inverse
        punit[spot, :] = unit
        prad[spot, :] = inverse
        embed = unit.astype(BF16)
        paug[spot, :DIM] = embed * jnp.array(inner_scale, BF16)
        ptr[:, spot] = embed.astype(F32).T.astype(BF16)

    def forward(b):
        power[b] = jnp.dot(paug[...], qbuf[b], preferred_element_type=F32)

        @pl.loop(0, PN // UNROLL)
        def _(step):
            for k in range(UNROLL):
                c = step * UNROLL + k
                spot = pl.ds(pl.multiple_of(c * PT, PT), PT)
                logits = power[b, spot, :]
                top = jnp.max(logits, axis=0, keepdims=True)
                powers = jnp.exp(logits - top)
                power[b, spot, :] = powers
                tops[b, pl.ds(c, 1), :] = top
                tots[b, pl.ds(c, 1), :] = jnp.sum(powers, axis=0, keepdims=True)

        kept = qbuf[b, DIM:DIM + TAIL, :].astype(F32)[1:2, :]
        keeps[b] = jnp.broadcast_to(kept, (TAIL, QR))
        best = (jnp.log(tots[b]) + tops[b]) * (1.0 / inner_scale) * kept
        high = best.astype(BF16)
        rest = best - high.astype(F32)
        middle = rest.astype(BF16)
        low = (rest - middle.astype(F32)).astype(BF16)
        sums = jnp.dot(
            jnp.concatenate([high, middle, low], axis=0), member[...], preferred_element_type=F32)
        scores = outer_scale * (sums[:TAIL] + (sums[TAIL:2 * TAIL] + sums[2 * TAIL:]))
        scores = jnp.where(exact_iota((TAIL, QR), 0) < PN, scores, hidden_out)
        score[b] = scores
        top = jnp.max(scores, axis=0, keepdims=True)
        total = top + jnp.log(jnp.sum(jnp.exp(scores - top), axis=0, keepdims=True))
        lse_own[pl.ds(b, 1), :] = total
        return total

    def to_grads(b, dscore):
        coef[...] = dscore * keeps[b] * (outer_scale * loss_scale) / tots[b]

        @pl.loop(0, PN // UNROLL)
        def _(step):
            for k in range(UNROLL):
                c = step * UNROLL + k
                spot = pl.ds(pl.multiple_of(c * PT, PT), PT)
                gsim[b, spot, :] = (power[b, spot, :] * coef[pl.ds(c, 1), :]).astype(BF16)

    def send_grad(b):
        return pltpu.make_async_remote_copy(
            src_ref=tq_out.at[b - 1], dst_ref=tq_in.at[b - 1], send_sem=ts.at[b - 1],
            recv_sem=tr.at[b - 1], device_id=ring[-b], device_id_type=MESH)

    def send_lse(n):
        return pltpu.make_async_remote_copy(
            src_ref=lse_own, dst_ref=lse_in.at[n], send_sem=ls.at[n], recv_sem=lr.at[n],
            device_id=ring[HOPS[n]], device_id_type=MESH)

    lse_own[...] = jnp.zeros(lse_own.shape, F32)
    own = [forward(0)]
    for b in (1, 2):
        send_query(b).wait_recv()
        own.append(forward(b))
    for n in range(4):
        send_lse(n).start()
    for b in (2, 1):
        to_grads(b, jnp.exp(score[b] - lse_own[b:b + 1, :]))
        tq_out[b - 1] = jnp.dot(ptr[...], gsim[b], preferred_element_type=F32).astype(BF16)
        send_grad(b).start()

    place = jnp.zeros((1, QR), jnp.int32)
    for q in range(QN):
        place = jnp.where(lane // QT == q, pos[q], place)
    onehot = jnp.where(exact_iota((TAIL, QR), 0) == place, 1.0, 0.0)

    for n in range(4):
        send_lse(n).wait_recv()
    totals = (
        log_sum((lse_own[0:1, :], lse_in[2, 1:2, :], lse_in[3, 2:3, :])),
        log_sum((lse_in[0, 0:1, :], lse_own[1:2, :], lse_in[2, 2:3, :])),
        log_sum((lse_in[1, 0:1, :], lse_in[0, 1:2, :], lse_own[2:3, :])),
    )
    loss_out[...] = totals[0] - jnp.sum(onehot * score[0], axis=0, keepdims=True)
    for b in (1, 2):
        factor = jnp.exp(lse_own[b:b + 1, :] - totals[b])
        qscaled[b - 1] = (qbuf[b, :DIM, :].astype(F32) * factor).astype(BF16)
    to_grads(0, jnp.exp(score[0] - totals[0]) - onehot)

    for r in range(PR // CHUNK):
        spot = pl.ds(r * CHUNK, CHUNK)
        grad = nt_dot(gsim[0, spot, :], qbuf[0, :DIM, :])
        grad += nt_dot(gsim[1, spot, :], qscaled[0])
        grad += nt_dot(gsim[2, spot, :], qscaled[1])
        unit = punit[spot, :]
        pre = (grad - unit * jnp.sum(unit * grad, axis=-1, keepdims=True)) * prad[spot, :]
        pre = pre.astype(BF16)
        ppre[spot, :] = pre
        pre_t[:, spot] = pre.astype(F32).T.astype(BF16)

    qgrad = jnp.dot(ptr[...], gsim[0], preferred_element_type=F32)
    send_grad(1).wait_recv()
    send_grad(2).wait_recv()
    qgrad += jnp.exp(lse_in[2, 1:2, :] - totals[0]) * tq_in[0].astype(F32)
    qgrad += jnp.exp(lse_in[3, 2:3, :] - totals[0]) * tq_in[1].astype(F32)
    unit = qunit[...]
    pre = (qgrad - unit * jnp.sum(unit * qgrad, axis=0, keepdims=True)) * qrad[...]
    pre = pre.astype(BF16)
    pre_t[:, whole_q] = pre

    def piece(first, size, j):
        return pl.ds(pl.multiple_of(first + j * size, size), size)

    def start(stage, peers, source, target, mine):
        for j, where in peers:
            pltpu.make_async_remote_copy(
                src_ref=source(j), dst_ref=target(mine), send_sem=push.at[stage],
                recv_sem=pull.at[stage], device_id=where, device_id_type=MESH).start()

    def bulk(stage, peers, whole):
        return pltpu.make_async_remote_copy(
            src_ref=whole, dst_ref=whole, send_sem=push.at[stage], recv_sem=pull.at[stage],
            device_id=peers[0][1], device_id_type=MESH)

    def added(box):
        return jnp.sum(box[...].astype(F32), axis=0).astype(BF16)

    along_y, along_z, along_x, across = (y_line, y), (z_line, z), (x_line, x), (partner, core)
    plan = (
        ((a1, a2, a3, a4), (along_y, along_z, along_x, across)),
        ((b1, b2, b3, b4), (along_z, along_y, along_x, across)),
        ((c1, c2, c3, c4), (along_x, along_y, along_z, across)),
    )
    share = HID // 3
    def arrived(n, hop):
        boxes, route = plan[n]
        peers = route[hop][0]
        bulk(5 * n + hop, peers, boxes[hop].at[pl.ds(0, len(peers))]).wait_recv()

    for n, (boxes, route) in enumerate(plan):
        peers, mine = route[0]
        size = boxes[0].shape[1]
        part = jnp.dot(pre_t[...], both[:, n * share:(n + 1) * share], preferred_element_type=F32)
        for t in range(share // DIM):
            src[n * share + t * DIM:n * share + (t + 1) * DIM, :] = (
                part[:, t * DIM:(t + 1) * DIM].astype(BF16))
        start(5 * n, peers, lambda j: src.at[piece(n * share, size, j)], lambda j: boxes[0].at[j], mine)
        boxes[0][mine] = src[piece(n * share, size, mine), :]

    def hidden_tile(r):
        spot = pl.ds(r * CHUNK, CHUNK)
        rows = pre_t[:, whole_q].astype(F32).T.astype(BF16) if r == PR // CHUNK else ppre[spot, :]
        hidden_out_ref[spot, :] = nt_dot(rows, proj[...]).astype(BF16)

    for hop in range(3):
        for r in (2 * hop, 2 * hop + 1):
            hidden_tile(r)
        for n, (boxes, route) in enumerate(plan):
            peers, here = route[hop + 1]
            box = boxes[hop + 1]
            arrived(n, hop)
            box[here] = added(boxes[hop])
            start(5 * n + hop + 1, peers, lambda j: box.at[here], lambda j: box.at[j], here)
    for n, (boxes, route) in enumerate(plan):
        peers, mine = route[0]
        size = boxes[0].shape[1]
        arrived(n, 3)
        gathered[piece(n * share, size, mine), :] = added(boxes[3])
        start(
            5 * n + 4, peers, lambda j: gathered.at[piece(n * share, size, mine)],
            lambda j: gathered.at[piece(n * share, size, j)], mine)

    def spread(n):
        boxes, route = plan[n]
        peers = route[0][0]
        return bulk(5 * n + 4, peers, gathered.at[pl.ds(n * share, len(peers) * boxes[0].shape[1])])

    for n in range(3):
        spread(n).wait_recv()
    total_out[...] = gathered[...]

    for n, (boxes, route) in enumerate(plan):
        for hop in range(4):
            peers = route[hop][0]
            bulk(5 * n + hop, peers, boxes[hop].at[pl.ds(0, len(peers))]).wait_send()
        spread(n).wait_send()
    for b in (1, 2):
        send_query(b).wait_send()
        send_grad(b).wait_send()
    for n in range(4):
        send_lse(n).wait_send()


def run_step(query_lengths, passage_lengths, positives, query_hidden, passage_hidden, projection):
    dma = pltpu.SemaphoreType.DMA
    vmem = pl.BlockSpec(memory_space=pltpu.VMEM)
    hbm = pl.BlockSpec(memory_space=pltpu.HBM)
    vm = pltpu.VMEM
    ny = NYH * NYL
    share = HID // 3
    return pl.pallas_call(
        step_kernel,
        out_shape=(
            jax.ShapeDtypeStruct((1, QR), F32),
            jax.ShapeDtypeStruct((PR + QR, HID), BF16),
            jax.ShapeDtypeStruct((HID, DIM), BF16),
        ),
        in_specs=[hbm] * 6,
        out_specs=(vmem, vmem, vmem),
        scratch_shapes=[
            pltpu.SMEM((QN,), jnp.int32), pltpu.SMEM((PN,), jnp.int32), pltpu.SMEM((QN,), jnp.int32),
            vm((PR + QR, HID), BF16), vm((HID, DIM), BF16),
            vm((3, QR, QR), BF16), vm((DIM, QR), F32), vm((1, QR), F32),
            vm((PR, 2 * DIM), BF16), vm((DIM, PR), BF16), vm((PR, DIM), F32), vm((PR, 1), F32),
            vm((3, PR, QR), F32), vm((3, PR, QR), BF16),
            vm((3, TAIL, QR), F32), vm((3, TAIL, QR), F32), vm((3, TAIL, QR), F32),
            vm((3, TAIL, QR), F32), vm((TAIL, QR), F32), vm((QR, QR), BF16),
            vm((8, QR), F32), vm((4, 8, QR), F32),
            vm((2, DIM, QR), BF16), vm((2, DIM, QR), BF16), vm((2, DIM, QR), BF16),
            vm((PR, DIM), BF16), vm((DIM, PR + QR), BF16),
            vm((HID, DIM), BF16),
            vm((ny, share // ny, DIM), BF16), vm((NZ, share // ny, DIM), BF16),
            vm((NX, share // ny, DIM), BF16), vm((NC, share // ny, DIM), BF16),
            vm((NZ, share // NZ, DIM), BF16), vm((ny, share // NZ, DIM), BF16),
            vm((NX, share // NZ, DIM), BF16), vm((NC, share // NZ, DIM), BF16),
            vm((NX, share // NX, DIM), BF16), vm((ny, share // NX, DIM), BF16),
            vm((NZ, share // NX, DIM), BF16), vm((NC, share // NX, DIM), BF16),
            vm((HID, DIM), BF16),
            dma((6,)), dma((2,)), dma((2,)), dma((4,)), dma((4,)), dma((2,)), dma((2,)),
            dma((15,)), dma((15,)),
        ],
        compiler_params=pltpu.CompilerParams(
            collective_id=0, has_side_effects=True, vmem_limit_bytes=24 * 1024 * 1024),
    )(query_lengths, passage_lengths, positives, query_hidden, passage_hidden, projection)


def finish_kernel(loss, hidden, total, loss_out, gq_any, gp_any, gproj, sem):
    put_p = pltpu.make_async_copy(hidden.at[pl.ds(0, PR)], gp_any, sem.at[0])
    put_q = pltpu.make_async_copy(hidden.at[pl.ds(PR, QR)], gq_any, sem.at[1])
    put_p.start()
    put_q.start()
    for q in range(QN):
        loss_out[q] = loss[0, q * QT]
    for n in range(HID // DIM):
        spot = pl.ds(n * DIM, DIM)
        gproj[spot, :] = total[spot, :].astype(F32).T * (1.0 / (NB * NMP))
    put_p.wait()
    put_q.wait()


def run_finish(loss, hidden, total):
    smem = pl.BlockSpec(memory_space=pltpu.SMEM)
    vmem = pl.BlockSpec(memory_space=pltpu.VMEM)
    hbm = pl.BlockSpec(memory_space=pl.ANY)
    return pl.pallas_call(
        finish_kernel,
        out_shape=(
            jax.ShapeDtypeStruct((QN,), F32),
            jax.ShapeDtypeStruct((QR, HID), BF16),
            jax.ShapeDtypeStruct((PR, HID), BF16),
            jax.ShapeDtypeStruct((HID, DIM), F32),
        ),
        in_specs=[smem, vmem, vmem],
        out_specs=(smem, hbm, hbm, vmem),
        scratch_shapes=[pltpu.SemaphoreType.DMA((2,))],
        compiler_params=pltpu.CompilerParams(vmem_limit_bytes=16 * 1024 * 1024),
    )(loss, hidden, total)


def per_device(query_hidden, passage_hidden, projection, query_lengths, passage_lengths, positives):
    loss, hidden, total = run_step(*(
        pltpu.with_memory_space_constraint(v, pltpu.HBM) for v in (
            query_lengths, passage_lengths, positives, query_hidden, passage_hidden, projection)))
    return run_finish(loss, hidden, total)


def solution(mesh):
    in_specs = (
        P(("batch", "mp"), None),
        P(("batch", "mp"), None),
        P(),
        P(("batch", "mp")),
        P(("batch", "mp")),
        P(("batch", "mp")),
    )
    out_specs = (P(("batch", "mp")), P(("batch", "mp"), None), P(("batch", "mp"), None), P())
    return jax.shard_map(
        per_device, mesh=mesh, in_specs=in_specs, out_specs=out_specs, check_vma=False
    )
```

```python
import jax
import jax.numpy as jnp
from jax import lax
from jax.experimental import pallas as pl
from jax.experimental.pallas import tpu as pltpu
from jax.sharding import PartitionSpec as P

inner_scale = 128.0
outer_scale = 8.0
loss_scale = 32.0
norm_eps = 1e-06
hidden_out = -1e30

NX, NZ, NYH, NYL, NC = 4, 8, 4, 2, 2
NMP = NYL * NC
NB = NX * NZ * NYH
MESH = pl.DeviceIdType.MESH
F32 = jnp.float32
BF16 = jnp.bfloat16
QN, QT, PN, PT = 8, 32, 10, 128
QR, PR, DIM, HID = QN * QT, PN * PT, 128, 768
TAIL = 16
HOPS = (1, 2, -1, -2)
LSE_READY = (1, 0, 2, 2)
CHUNK = 256
UNROLL = 2


def exact_iota(shape, axis):
    return lax.broadcasted_iota(jnp.int32, shape, axis)


def nt_dot(left, right):
    return lax.dot_general(left, right, (((1,), (1,)), ((), ())), preferred_element_type=F32)


def log_sum(rows):
    top = jnp.maximum(jnp.maximum(rows[0], rows[1]), rows[2])
    return top + jnp.log(jnp.exp(rows[0] - top) + jnp.exp(rows[1] - top) + jnp.exp(rows[2] - top))


def turned(here, count):
    order = sorted(range(count), key=lambda a: -min(a, count - a))
    spots = []
    for a in order:
        there = here + a
        spots.append((a, jnp.where(there >= count, there - count, there) if a else here))
    return spots


def step_kernel(
    qlen_any, plen_any, pos_any, qh_any, ph_any, proj_any,
    loss_out, hidden_out_ref, total_out,
    qlen, plen, pos, both, proj, qbuf, qunit, qrad, paug, ptr, punit, prad, power, gsim,
    tops, tots, score, keeps, coef, member, lse_own, lse_in, tq_out, tq_in, qscaled,
    ppre, pre_t, pgrad, ppart, src, a1, a2, a3, a4, b1, b2, b3, b4, c1, c2, c3, c4, gathered,
    in_sem, qs, qr, ls, lr, ts, tr, push, pull,
):
    bi = lax.axis_index("batch")
    mi = lax.axis_index("mp")
    yh = lax.rem(bi, NYH)
    up = lax.div(bi, NYH)
    z = lax.rem(up, NZ)
    x = lax.div(up, NZ)
    yl = lax.div(mi, NC)
    core = lax.rem(mi, NC)
    y = yh * NYL + yl
    xz = bi - yh

    def at_y(spot):
        return (xz + lax.div(spot, NYL), lax.rem(spot, NYL) * NC + core)

    def at_z(spot):
        return (bi + (spot - z) * NYH, mi)

    def at_x(spot):
        return (bi + (spot - x) * (NYH * NZ), mi)

    def line(here, count, place):
        return [(spot, place(spot)) for a, spot in turned(here, count) if a]

    def ring_peer(hop):
        there = bi + hop
        there = jnp.where(there >= NB, there - NB, there) if hop > 0 else jnp.where(there < 0, there + NB, there)
        return (there, mi)

    ring = {hop: ring_peer(hop) for hop in HOPS}

    whole_p, whole_q = pl.ds(0, PR), pl.ds(PR, QR)
    get_proj = pltpu.make_async_copy(proj_any, proj, in_sem.at[0])
    get_qh = pltpu.make_async_copy(qh_any, both.at[whole_q], in_sem.at[1])
    get_ph = pltpu.make_async_copy(ph_any, both.at[whole_p], in_sem.at[2])

    small = [
        pltpu.make_async_copy(far, near, in_sem.at[3 + n])
        for n, (far, near) in enumerate(((qlen_any, qlen), (plen_any, plen), (pos_any, pos)))]

    @pl.when(bi >= 0)
    def _():
        for copy in small:
            copy.start()
        get_proj.start()
        get_qh.start()
        get_ph.start()

    barrier = pltpu.get_barrier_semaphore()

    def greet(places):
        for where in places:
            pl.semaphore_signal(barrier, inc=1, device_id=where, device_id_type=MESH)
        return len(places)

    greeted = greet([ring[hop] for hop in HOPS])
    y_line = line(y, NYH * NYL, at_y)
    z_line = line(z, NZ, at_z)
    x_line = line(x, NX, at_x)
    partner = [(NC - 1 - core, (bi, mi + (NC - 1 - 2 * core)))]
    greeted += greet([where for _, where in y_line + z_line + x_line + partner])

    for copy in small:
        copy.wait()
    lane = exact_iota((1, QR), 1)
    keep = jnp.zeros((1, QR), F32)
    for q in range(QN):
        token = lane - q * QT
        keep = jnp.where((token >= 0) & (token < qlen[q]), 1.0, keep)
    tail_row = exact_iota((TAIL, QR), 0)
    qbuf[0, DIM:DIM + TAIL, :] = jnp.where(
        tail_row == 0, 1.0, jnp.where(tail_row == 1, keep, 0.0)).astype(BF16)
    for b in range(3):
        qbuf[b, DIM + TAIL:, :] = jnp.zeros((QR - DIM - TAIL, QR), BF16)

    get_proj.wait()
    get_qh.wait()
    before = jnp.dot(both[whole_q, :], proj[...], preferred_element_type=F32).T
    radius = jnp.sqrt(jnp.sum(before * before, axis=0, keepdims=True) + norm_eps)
    inverse = 1.0 / radius
    unit = before * inverse
    qunit[...] = unit
    qrad[...] = inverse
    qbuf[0, :DIM, :] = unit.astype(BF16)

    pl.semaphore_wait(barrier, greeted)

    def send_query(b):
        part = pl.ds(0, DIM + TAIL)
        return pltpu.make_async_remote_copy(
            src_ref=qbuf.at[0, part], dst_ref=qbuf.at[b, part], send_sem=qs.at[b - 1],
            recv_sem=qr.at[b - 1], device_id=ring[b], device_id_type=MESH)

    send_query(2).start()
    send_query(1).start()

    member[...] = jnp.where(
        exact_iota((QR, QR), 0) // QT == exact_iota((QR, QR), 1) // QT, 1.0, 0.0).astype(BF16)
    tops[...] = jnp.zeros(tops.shape, F32)
    tots[...] = jnp.ones(tots.shape, F32)

    @pl.loop(0, PN)
    def _(c):
        spot = pl.ds(pl.multiple_of(c * PT, PT), PT)
        outside = (exact_iota((PT, DIM), 0) >= plen[c]) & (exact_iota((PT, DIM), 1) == 0)
        paug[spot, DIM:] = jnp.where(outside, hidden_out, 0.0).astype(BF16)

    get_ph.wait()

    for r in range(PR // CHUNK):
        spot = pl.ds(r * CHUNK, CHUNK)
        before = jnp.dot(both[spot, :], proj[...], preferred_element_type=F32)
        radius = jnp.sqrt(jnp.sum(before * before, axis=-1, keepdims=True) + norm_eps)
        inverse = 1.0 / radius
        unit = before * inverse
        punit[spot, :] = unit
        prad[spot, :] = inverse
        embed = unit.astype(BF16)
        paug[spot, :DIM] = embed * jnp.array(inner_scale, BF16)
        ptr[:, spot] = embed.astype(F32).T.astype(BF16)

    def forward(b):
        power[b] = jnp.dot(paug[...], qbuf[b], preferred_element_type=F32)

        @pl.loop(0, PN // UNROLL)
        def _(step):
            for k in range(UNROLL):
                c = step * UNROLL + k
                spot = pl.ds(pl.multiple_of(c * PT, PT), PT)
                logits = power[b, spot, :]
                top = jnp.max(logits, axis=0, keepdims=True)
                powers = jnp.exp(logits - top)
                power[b, spot, :] = powers
                tops[b, pl.ds(c, 1), :] = top
                tots[b, pl.ds(c, 1), :] = jnp.sum(powers, axis=0, keepdims=True)

        kept = qbuf[b, DIM:DIM + TAIL, :].astype(F32)[1:2, :]
        keeps[b] = jnp.broadcast_to(kept, (TAIL, QR))
        best = (jnp.log(tots[b]) + tops[b]) * (1.0 / inner_scale) * kept
        high = best.astype(BF16)
        rest = best - high.astype(F32)
        middle = rest.astype(BF16)
        low = (rest - middle.astype(F32)).astype(BF16)
        sums = jnp.dot(
            jnp.concatenate([high, middle, low], axis=0), member[...], preferred_element_type=F32)
        scores = outer_scale * (sums[:TAIL] + (sums[TAIL:2 * TAIL] + sums[2 * TAIL:]))
        scores = jnp.where(exact_iota((TAIL, QR), 0) < PN, scores, hidden_out)
        score[b] = scores
        top = jnp.max(scores, axis=0, keepdims=True)
        total = top + jnp.log(jnp.sum(jnp.exp(scores - top), axis=0, keepdims=True))
        for k in range(b, 3):
            lse_own[k, b:b + 1, :] = total

    def to_grads(b, dscore):
        coef[...] = dscore * keeps[b] * (outer_scale * loss_scale) / tots[b]

        @pl.loop(0, PN // UNROLL)
        def _(step):
            for k in range(UNROLL):
                c = step * UNROLL + k
                spot = pl.ds(pl.multiple_of(c * PT, PT), PT)
                gsim[b, spot, :] = (power[b, spot, :] * coef[pl.ds(c, 1), :]).astype(BF16)

    def send_grad(b):
        return pltpu.make_async_remote_copy(
            src_ref=tq_out.at[b - 1], dst_ref=tq_in.at[b - 1], send_sem=ts.at[b - 1],
            recv_sem=tr.at[b - 1], device_id=ring[-b], device_id_type=MESH)

    def send_lse(n):
        return pltpu.make_async_remote_copy(
            src_ref=lse_own.at[LSE_READY[n]], dst_ref=lse_in.at[n], send_sem=ls.at[n], recv_sem=lr.at[n],
            device_id=ring[HOPS[n]], device_id_type=MESH)

    lse_own[...] = jnp.zeros(lse_own.shape, F32)
    for b in range(3):
        if b:
            send_query(b).wait_recv()
        forward(b)
        for n in range(4):
            if LSE_READY[n] == b:
                send_lse(n).start()
    for b in (2, 1):
        to_grads(b, jnp.exp(score[b] - lse_own[2, b:b + 1, :]))
        tq_out[b - 1] = jnp.dot(ptr[...], gsim[b], preferred_element_type=F32).astype(BF16)
        send_grad(b).start()

    place = jnp.zeros((1, QR), jnp.int32)
    for q in range(QN):
        place = jnp.where(lane // QT == q, pos[q], place)
    onehot = jnp.where(exact_iota((TAIL, QR), 0) == place, 1.0, 0.0)

    def scaled(b, rows):
        factor = jnp.exp(lse_own[2, b:b + 1, :] - log_sum(rows))
        qscaled[b - 1] = (qbuf[b, :DIM, :].astype(F32) * factor).astype(BF16)

    send_lse(0).wait_recv()
    send_lse(1).wait_recv()
    scaled(2, (lse_in[1, 0:1, :], lse_in[0, 1:2, :], lse_own[2, 2:3, :]))
    pgrad[...] = nt_dot(gsim[2], qscaled[1])
    send_lse(2).wait_recv()
    scaled(1, (lse_in[0, 0:1, :], lse_own[2, 1:2, :], lse_in[2, 2:3, :]))
    pgrad[...] += nt_dot(gsim[1], qscaled[0])
    send_lse(3).wait_recv()
    total = log_sum((lse_own[2, 0:1, :], lse_in[2, 1:2, :], lse_in[3, 2:3, :]))
    to_grads(0, jnp.exp(score[0] - total) - onehot)

    for r in range(PR // CHUNK):
        spot = pl.ds(r * CHUNK, CHUNK)
        grad = pgrad[spot, :] + nt_dot(gsim[0, spot, :], qbuf[0, :DIM, :])
        unit = punit[spot, :]
        pre = (grad - unit * jnp.sum(unit * grad, axis=-1, keepdims=True)) * prad[spot, :]
        pre = pre.astype(BF16)
        ppre[spot, :] = pre
        pre_t[:, spot] = pre.astype(F32).T.astype(BF16)

    ppart[...] = jnp.dot(pre_t[:, whole_p], both[whole_p, :], preferred_element_type=F32)
    qgrad = jnp.dot(ptr[...], gsim[0], preferred_element_type=F32)

    send_grad(1).wait_recv()
    send_grad(2).wait_recv()
    qgrad += jnp.exp(lse_in[2, 1:2, :] - total) * tq_in[0].astype(F32)
    qgrad += jnp.exp(lse_in[3, 2:3, :] - total) * tq_in[1].astype(F32)
    unit = qunit[...]
    pre = (qgrad - unit * jnp.sum(unit * qgrad, axis=0, keepdims=True)) * qrad[...]
    pre = pre.astype(BF16)
    pre_t[:, whole_q] = pre

    def piece(first, size, j):
        return pl.ds(pl.multiple_of(first + j * size, size), size)

    def start(stage, peers, source, target, mine):
        for j, where in peers:
            pltpu.make_async_remote_copy(
                src_ref=source(j), dst_ref=target(mine), send_sem=push.at[stage],
                recv_sem=pull.at[stage], device_id=where, device_id_type=MESH).start()

    def bulk(stage, peers, whole):
        return pltpu.make_async_remote_copy(
            src_ref=whole, dst_ref=whole, send_sem=push.at[stage], recv_sem=pull.at[stage],
            device_id=peers[0][1], device_id_type=MESH)

    def added(box):
        return jnp.sum(box[...].astype(F32), axis=0).astype(BF16)

    along_y, along_z, along_x, across = (y_line, y), (z_line, z), (x_line, x), (partner, core)
    plan = (
        ((a1, a2, a3, a4), (along_y, along_z, along_x, across)),
        ((b1, b2, b3, b4), (along_z, along_y, along_x, across)),
        ((c1, c2, c3, c4), (along_x, along_y, along_z, across)),
    )
    share = HID // 3
    def arrived(n, hop):
        boxes, route = plan[n]
        peers = route[hop][0]
        bulk(5 * n + hop, peers, boxes[hop].at[pl.ds(0, len(peers))]).wait_recv()

    for n, (boxes, route) in enumerate(plan):
        peers, mine = route[0]
        size = boxes[0].shape[1]
        columns = pl.ds(n * share, share)
        part = ppart[:, columns] + jnp.dot(pre, both[whole_q, columns], preferred_element_type=F32)
        for t in range(share // DIM):
            src[n * share + t * DIM:n * share + (t + 1) * DIM, :] = (
                part[:, t * DIM:(t + 1) * DIM].astype(BF16))
        start(5 * n, peers, lambda j: src.at[piece(n * share, size, j)], lambda j: boxes[0].at[j], mine)
        boxes[0][mine] = src[piece(n * share, size, mine), :]

    def hidden_tile(r):
        spot = pl.ds(r * CHUNK, CHUNK)
        rows = pre_t[:, whole_q].astype(F32).T.astype(BF16) if r == PR // CHUNK else ppre[spot, :]
        hidden_out_ref[spot, :] = nt_dot(rows, proj[...]).astype(BF16)

    def onward(n, hop):
        boxes, route = plan[n]
        peers, here = route[hop + 1]
        box = boxes[hop + 1]
        arrived(n, hop)
        box[here] = added(boxes[hop])
        start(5 * n + hop + 1, peers, lambda j: box.at[here], lambda j: box.at[j], here)

    def share_out(n):
        boxes, route = plan[n]
        peers, mine = route[0]
        size = boxes[0].shape[1]
        arrived(n, 3)
        gathered[piece(n * share, size, mine), :] = added(boxes[3])
        start(
            5 * n + 4, peers, lambda j: gathered.at[piece(n * share, size, mine)],
            lambda j: gathered.at[piece(n * share, size, j)], mine)

    loss = total - jnp.sum(onehot * score[0], axis=0, keepdims=True)
    for q in range(QN):
        loss_out[q] = jnp.sum(jnp.where(lane == q * QT, loss, 0.0))
    hidden_tile(0)
    hidden_tile(1)
    for n in range(3):
        onward(n, 0)
    hidden_tile(2)
    hidden_tile(3)
    for n in (2, 0, 1):
        onward(n, 1)
    hidden_tile(4)
    hidden_tile(5)
    for n in (0, 1):
        onward(n, 2)
    for n in (0, 1):
        share_out(n)
    onward(2, 2)
    share_out(2)

    def spread(n):
        boxes, route = plan[n]
        peers = route[0][0]
        return bulk(5 * n + 4, peers, gathered.at[pl.ds(n * share, len(peers) * boxes[0].shape[1])])

    for n in range(3):
        spread(n).wait_recv()
    total_out[...] = gathered[...]

    for n, (boxes, route) in enumerate(plan):
        for hop in range(4):
            peers = route[hop][0]
            bulk(5 * n + hop, peers, boxes[hop].at[pl.ds(0, len(peers))]).wait_send()
        spread(n).wait_send()
    for b in (1, 2):
        send_query(b).wait_send()
        send_grad(b).wait_send()
    for n in range(4):
        send_lse(n).wait_send()


def run_step(query_lengths, passage_lengths, positives, query_hidden, passage_hidden, projection):
    dma = pltpu.SemaphoreType.DMA
    vmem = pl.BlockSpec(memory_space=pltpu.VMEM)
    hbm = pl.BlockSpec(memory_space=pltpu.HBM)
    vm = pltpu.VMEM
    ny = NYH * NYL
    share = HID // 3
    return pl.pallas_call(
        step_kernel,
        out_shape=(
            jax.ShapeDtypeStruct((QN,), F32),
            jax.ShapeDtypeStruct((PR + QR, HID), BF16),
            jax.ShapeDtypeStruct((HID, DIM), BF16),
        ),
        in_specs=[hbm] * 6,
        out_specs=(pl.BlockSpec(memory_space=pltpu.SMEM), vmem, vmem),
        scratch_shapes=[
            pltpu.SMEM((QN,), jnp.int32), pltpu.SMEM((PN,), jnp.int32), pltpu.SMEM((QN,), jnp.int32),
            vm((PR + QR, HID), BF16), vm((HID, DIM), BF16),
            vm((3, QR, QR), BF16), vm((DIM, QR), F32), vm((1, QR), F32),
            vm((PR, 2 * DIM), BF16), vm((DIM, PR), BF16), vm((PR, DIM), F32), vm((PR, 1), F32),
            vm((3, PR, QR), F32), vm((3, PR, QR), BF16),
            vm((3, TAIL, QR), F32), vm((3, TAIL, QR), F32), vm((3, TAIL, QR), F32),
            vm((3, TAIL, QR), F32), vm((TAIL, QR), F32), vm((QR, QR), BF16),
            vm((3, 8, QR), F32), vm((4, 8, QR), F32),
            vm((2, DIM, QR), BF16), vm((2, DIM, QR), BF16), vm((2, DIM, QR), BF16),
            vm((PR, DIM), BF16), vm((DIM, PR + QR), BF16),
            vm((PR, DIM), F32), vm((DIM, HID), F32),
            vm((HID, DIM), BF16),
            vm((ny, share // ny, DIM), BF16), vm((NZ, share // ny, DIM), BF16),
            vm((NX, share // ny, DIM), BF16), vm((NC, share // ny, DIM), BF16),
            vm((NZ, share // NZ, DIM), BF16), vm((ny, share // NZ, DIM), BF16),
            vm((NX, share // NZ, DIM), BF16), vm((NC, share // NZ, DIM), BF16),
            vm((NX, share // NX, DIM), BF16), vm((ny, share // NX, DIM), BF16),
            vm((NZ, share // NX, DIM), BF16), vm((NC, share // NX, DIM), BF16),
            vm((HID, DIM), BF16),
            dma((6,)), dma((2,)), dma((2,)), dma((4,)), dma((4,)), dma((2,)), dma((2,)),
            dma((15,)), dma((15,)),
        ],
        compiler_params=pltpu.CompilerParams(
            collective_id=0, has_side_effects=True, vmem_limit_bytes=24 * 1024 * 1024),
    )(query_lengths, passage_lengths, positives, query_hidden, passage_hidden, projection)


def finish_kernel(loss, hidden, total, loss_any, gq_any, gp_any, gproj_any, gproj, sem):
    puts = [
        pltpu.make_async_copy(near, far, sem.at[n])
        for n, (near, far) in enumerate((
            (hidden.at[pl.ds(0, PR)], gp_any), (hidden.at[pl.ds(PR, QR)], gq_any),
            (loss, loss_any), (gproj, gproj_any)))]
    for put in puts[:3]:
        put.start()
    for n in range(HID // DIM):
        spot = pl.ds(n * DIM, DIM)
        gproj[spot, :] = total[spot, :].astype(F32).T * (1.0 / (NB * NMP))
    puts[3].start()
    for put in puts:
        put.wait()


def run_finish(loss, hidden, total):
    vmem = pl.BlockSpec(memory_space=pltpu.VMEM)
    hbm = pl.BlockSpec(memory_space=pl.ANY)
    return pl.pallas_call(
        finish_kernel,
        out_shape=(
            jax.ShapeDtypeStruct((QN,), F32),
            jax.ShapeDtypeStruct((QR, HID), BF16),
            jax.ShapeDtypeStruct((PR, HID), BF16),
            jax.ShapeDtypeStruct((HID, DIM), F32),
        ),
        in_specs=[hbm, vmem, vmem],
        out_specs=(hbm, hbm, hbm, hbm),
        scratch_shapes=[pltpu.VMEM((HID, DIM), F32), pltpu.SemaphoreType.DMA((4,))],
        compiler_params=pltpu.CompilerParams(vmem_limit_bytes=16 * 1024 * 1024),
    )(loss, hidden, total)


def per_device(query_hidden, passage_hidden, projection, query_lengths, passage_lengths, positives):
    loss, hidden, total = run_step(*(
        pltpu.with_memory_space_constraint(v, pltpu.HBM) for v in (
            query_lengths, passage_lengths, positives, query_hidden, passage_hidden, projection)))
    return run_finish(loss, hidden, total)


def solution(mesh):
    in_specs = (
        P(("batch", "mp"), None),
        P(("batch", "mp"), None),
        P(),
        P(("batch", "mp")),
        P(("batch", "mp")),
        P(("batch", "mp")),
    )
    out_specs = (P(("batch", "mp")), P(("batch", "mp"), None), P(("batch", "mp"), None), P())
    return jax.shard_map(
        per_device, mesh=mesh, in_specs=in_specs, out_specs=out_specs, check_vma=False
    )
```

```python
import jax
import jax.numpy as jnp
from jax import lax
from jax.experimental import pallas as pl
from jax.experimental.pallas import tpu as pltpu
from jax.sharding import PartitionSpec as P

inner_scale = 128.0
outer_scale = 8.0
loss_scale = 32.0
norm_eps = 1e-06
hidden_out = -1e30

NX, NZ, NYH, NYL, NC = 4, 8, 4, 2, 2
NMP = NYL * NC
NB = NX * NZ * NYH
MESH = pl.DeviceIdType.MESH
F32 = jnp.float32
BF16 = jnp.bfloat16
QN, QT, PN, PT = 8, 32, 10, 128
QR, PR, DIM, HID = QN * QT, PN * PT, 128, 768
TAIL = 16
HOPS = (1, 2, -1, -2)
LSE_READY = (1, 0, 2, 2)
CHUNK = 256
UNROLL = 2


def exact_iota(shape, axis):
    return lax.broadcasted_iota(jnp.int32, shape, axis)


def nt_dot(left, right):
    return lax.dot_general(left, right, (((1,), (1,)), ((), ())), preferred_element_type=F32)


def log_sum(rows):
    top = jnp.maximum(jnp.maximum(rows[0], rows[1]), rows[2])
    return top + jnp.log(jnp.exp(rows[0] - top) + jnp.exp(rows[1] - top) + jnp.exp(rows[2] - top))


def turned(here, count):
    order = sorted(range(count), key=lambda a: -min(a, count - a))
    spots = []
    for a in order:
        there = here + a
        spots.append((a, jnp.where(there >= count, there - count, there) if a else here))
    return spots


def step_kernel(
    qlen_any, plen_any, pos_any, qh_any, ph_any, proj_any,
    loss_out, hidden_out_ref, total_out,
    qlen, plen, pos, both, proj, qbuf, qunit, qrad, paug, ptr, punit, prad, power, gsim,
    tops, tots, score, keeps, coef, member, lse_own, lse_in, tq_out, tq_in, qscaled,
    ppre, pre_t, pgrad, ppart, src, a1, a2, a3, b1, b2, b3, c1, c2, c3, gathered,
    in_sem, qs, qr, ls, lr, ts, tr, push, pull,
):
    bi = lax.axis_index("batch")
    mi = lax.axis_index("mp")
    yh = lax.rem(bi, NYH)
    up = lax.div(bi, NYH)
    z = lax.rem(up, NZ)
    x = lax.div(up, NZ)
    yl = lax.div(mi, NC)
    core = lax.rem(mi, NC)
    y = yh * NYL + yl
    xz = bi - yh

    cores = turned(core, NC)

    def at_y(spot, side):
        return (xz + lax.div(spot, NYL), lax.rem(spot, NYL) * NC + side)

    def at_z(spot, side):
        return (bi + (spot - z) * NYH, mi + (side - core))

    def at_x(spot, side):
        return (bi + (spot - x) * (NYH * NZ), mi + (side - core))

    def pairs(here, count, place):
        return [
            (spot * NC + side, place(spot, side))
            for a, spot in turned(here, count) for c, side in cores if a or c]

    def line(here, count, place):
        return [(spot, place(spot, core)) for a, spot in turned(here, count) if a]

    def ring_peer(hop):
        there = bi + hop
        there = jnp.where(there >= NB, there - NB, there) if hop > 0 else jnp.where(there < 0, there + NB, there)
        return (there, mi)

    ring = {hop: ring_peer(hop) for hop in HOPS}

    whole_p, whole_q = pl.ds(0, PR), pl.ds(PR, QR)
    get_proj = pltpu.make_async_copy(proj_any, proj, in_sem.at[0])
    get_qh = pltpu.make_async_copy(qh_any, both.at[whole_q], in_sem.at[1])
    get_ph = pltpu.make_async_copy(ph_any, both.at[whole_p], in_sem.at[2])

    small = [
        pltpu.make_async_copy(far, near, in_sem.at[3 + n])
        for n, (far, near) in enumerate(((qlen_any, qlen), (plen_any, plen), (pos_any, pos)))]

    @pl.when(bi >= 0)
    def _():
        for copy in small:
            copy.start()
        get_proj.start()
        get_qh.start()
        get_ph.start()

    barrier = pltpu.get_barrier_semaphore()

    def greet(places):
        for where in places:
            pl.semaphore_signal(barrier, inc=1, device_id=where, device_id_type=MESH)
        return len(places)

    greeted = greet([ring[hop] for hop in HOPS])
    y_pairs = pairs(y, NYH * NYL, at_y)
    z_pairs = pairs(z, NZ, at_z)
    x_pairs = pairs(x, NX, at_x)
    y_line = line(y, NYH * NYL, at_y)
    z_line = line(z, NZ, at_z)
    x_line = line(x, NX, at_x)
    greeted += greet([where for _, where in y_pairs + z_pairs + x_pairs])

    for copy in small:
        copy.wait()
    lane = exact_iota((1, QR), 1)
    keep = jnp.zeros((1, QR), F32)
    for q in range(QN):
        token = lane - q * QT
        keep = jnp.where((token >= 0) & (token < qlen[q]), 1.0, keep)
    tail_row = exact_iota((TAIL, QR), 0)
    qbuf[0, DIM:DIM + TAIL, :] = jnp.where(
        tail_row == 0, 1.0, jnp.where(tail_row == 1, keep, 0.0)).astype(BF16)
    for b in range(3):
        qbuf[b, DIM + TAIL:, :] = jnp.zeros((QR - DIM - TAIL, QR), BF16)

    get_proj.wait()
    get_qh.wait()
    before = jnp.dot(both[whole_q, :], proj[...], preferred_element_type=F32).T
    radius = jnp.sqrt(jnp.sum(before * before, axis=0, keepdims=True) + norm_eps)
    inverse = 1.0 / radius
    unit = before * inverse
    qunit[...] = unit
    qrad[...] = inverse
    qbuf[0, :DIM, :] = unit.astype(BF16)

    pl.semaphore_wait(barrier, greeted)

    def send_query(b):
        part = pl.ds(0, DIM + TAIL)
        return pltpu.make_async_remote_copy(
            src_ref=qbuf.at[0, part], dst_ref=qbuf.at[b, part], send_sem=qs.at[b - 1],
            recv_sem=qr.at[b - 1], device_id=ring[b], device_id_type=MESH)

    send_query(2).start()
    send_query(1).start()

    member[...] = jnp.where(
        exact_iota((QR, QR), 0) // QT == exact_iota((QR, QR), 1) // QT, 1.0, 0.0).astype(BF16)
    tops[...] = jnp.zeros(tops.shape, F32)
    tots[...] = jnp.ones(tots.shape, F32)

    @pl.loop(0, PN)
    def _(c):
        spot = pl.ds(pl.multiple_of(c * PT, PT), PT)
        outside = (exact_iota((PT, DIM), 0) >= plen[c]) & (exact_iota((PT, DIM), 1) == 0)
        paug[spot, DIM:] = jnp.where(outside, hidden_out, 0.0).astype(BF16)

    get_ph.wait()

    for r in range(PR // CHUNK):
        spot = pl.ds(r * CHUNK, CHUNK)
        before = jnp.dot(both[spot, :], proj[...], preferred_element_type=F32)
        radius = jnp.sqrt(jnp.sum(before * before, axis=-1, keepdims=True) + norm_eps)
        inverse = 1.0 / radius
        unit = before * inverse
        punit[spot, :] = unit
        prad[spot, :] = inverse
        embed = unit.astype(BF16)
        paug[spot, :DIM] = embed * jnp.array(inner_scale, BF16)
        ptr[:, spot] = embed.astype(F32).T.astype(BF16)

    def forward(b):
        power[b] = jnp.dot(paug[...], qbuf[b], preferred_element_type=F32)

        @pl.loop(0, PN // UNROLL)
        def _(step):
            for k in range(UNROLL):
                c = step * UNROLL + k
                spot = pl.ds(pl.multiple_of(c * PT, PT), PT)
                logits = power[b, spot, :]
                top = jnp.max(logits, axis=0, keepdims=True)
                powers = jnp.exp(logits - top)
                power[b, spot, :] = powers
                tops[b, pl.ds(c, 1), :] = top
                tots[b, pl.ds(c, 1), :] = jnp.sum(powers, axis=0, keepdims=True)

        kept = qbuf[b, DIM:DIM + TAIL, :].astype(F32)[1:2, :]
        keeps[b] = jnp.broadcast_to(kept, (TAIL, QR))
        best = (jnp.log(tots[b]) + tops[b]) * (1.0 / inner_scale) * kept
        high = best.astype(BF16)
        rest = best - high.astype(F32)
        middle = rest.astype(BF16)
        low = (rest - middle.astype(F32)).astype(BF16)
        sums = jnp.dot(
            jnp.concatenate([high, middle, low], axis=0), member[...], preferred_element_type=F32)
        scores = outer_scale * (sums[:TAIL] + (sums[TAIL:2 * TAIL] + sums[2 * TAIL:]))
        scores = jnp.where(exact_iota((TAIL, QR), 0) < PN, scores, hidden_out)
        score[b] = scores
        top = jnp.max(scores, axis=0, keepdims=True)
        total = top + jnp.log(jnp.sum(jnp.exp(scores - top), axis=0, keepdims=True))
        for k in range(b, 3):
            lse_own[k, b:b + 1, :] = total

    def to_grads(b, dscore):
        coef[...] = dscore * keeps[b] * (outer_scale * loss_scale) / tots[b]

        @pl.loop(0, PN // UNROLL)
        def _(step):
            for k in range(UNROLL):
                c = step * UNROLL + k
                spot = pl.ds(pl.multiple_of(c * PT, PT), PT)
                gsim[b, spot, :] = (power[b, spot, :] * coef[pl.ds(c, 1), :]).astype(BF16)

    def send_grad(b):
        return pltpu.make_async_remote_copy(
            src_ref=tq_out.at[b - 1], dst_ref=tq_in.at[b - 1], send_sem=ts.at[b - 1],
            recv_sem=tr.at[b - 1], device_id=ring[-b], device_id_type=MESH)

    def send_lse(n):
        return pltpu.make_async_remote_copy(
            src_ref=lse_own.at[LSE_READY[n]], dst_ref=lse_in.at[n], send_sem=ls.at[n], recv_sem=lr.at[n],
            device_id=ring[HOPS[n]], device_id_type=MESH)

    lse_own[...] = jnp.zeros(lse_own.shape, F32)
    for b in range(3):
        if b:
            send_query(b).wait_recv()
        forward(b)
        for n in range(4):
            if LSE_READY[n] == b:
                send_lse(n).start()
    for b in (2, 1):
        to_grads(b, jnp.exp(score[b] - lse_own[2, b:b + 1, :]))
        tq_out[b - 1] = jnp.dot(ptr[...], gsim[b], preferred_element_type=F32).astype(BF16)
        send_grad(b).start()

    place = jnp.zeros((1, QR), jnp.int32)
    for q in range(QN):
        place = jnp.where(lane // QT == q, pos[q], place)
    onehot = jnp.where(exact_iota((TAIL, QR), 0) == place, 1.0, 0.0)

    def scaled(b, rows):
        factor = jnp.exp(lse_own[2, b:b + 1, :] - log_sum(rows))
        qscaled[b - 1] = (qbuf[b, :DIM, :].astype(F32) * factor).astype(BF16)

    send_lse(0).wait_recv()
    send_lse(1).wait_recv()
    scaled(2, (lse_in[1, 0:1, :], lse_in[0, 1:2, :], lse_own[2, 2:3, :]))
    pgrad[...] = nt_dot(gsim[2], qscaled[1])
    send_lse(2).wait_recv()
    scaled(1, (lse_in[0, 0:1, :], lse_own[2, 1:2, :], lse_in[2, 2:3, :]))
    pgrad[...] += nt_dot(gsim[1], qscaled[0])
    send_lse(3).wait_recv()
    total = log_sum((lse_own[2, 0:1, :], lse_in[2, 1:2, :], lse_in[3, 2:3, :]))
    to_grads(0, jnp.exp(score[0] - total) - onehot)

    for r in range(PR // CHUNK):
        spot = pl.ds(r * CHUNK, CHUNK)
        grad = pgrad[spot, :] + nt_dot(gsim[0, spot, :], qbuf[0, :DIM, :])
        unit = punit[spot, :]
        pre = (grad - unit * jnp.sum(unit * grad, axis=-1, keepdims=True)) * prad[spot, :]
        pre = pre.astype(BF16)
        ppre[spot, :] = pre
        pre_t[:, spot] = pre.astype(F32).T.astype(BF16)

    ppart[...] = jnp.dot(pre_t[:, whole_p], both[whole_p, :], preferred_element_type=F32)
    qgrad = jnp.dot(ptr[...], gsim[0], preferred_element_type=F32)

    send_grad(1).wait_recv()
    send_grad(2).wait_recv()
    qgrad += jnp.exp(lse_in[2, 1:2, :] - total) * tq_in[0].astype(F32)
    qgrad += jnp.exp(lse_in[3, 2:3, :] - total) * tq_in[1].astype(F32)
    unit = qunit[...]
    pre = (qgrad - unit * jnp.sum(unit * qgrad, axis=0, keepdims=True)) * qrad[...]
    pre = pre.astype(BF16)
    pre_t[:, whole_q] = pre

    def piece(first, size, j):
        return pl.ds(pl.multiple_of(first + j * size, size), size)

    def start(stage, peers, source, target, mine):
        for j, where in peers:
            pltpu.make_async_remote_copy(
                src_ref=source(j), dst_ref=target(mine), send_sem=push.at[stage],
                recv_sem=pull.at[stage], device_id=where, device_id_type=MESH).start()

    def bulk(stage, peers, whole):
        return pltpu.make_async_remote_copy(
            src_ref=whole, dst_ref=whole, send_sem=push.at[stage], recv_sem=pull.at[stage],
            device_id=peers[0][1], device_id_type=MESH)

    def added(box):
        return jnp.sum(box[...].astype(F32), axis=0).astype(BF16)

    along_y, along_z, along_x = (y_line, y), (z_line, z), (x_line, x)
    plan = (
        ((c1, c2, c3), ((x_pairs, x * NC + core), along_y, along_z)),
        ((a1, a2, a3), ((y_pairs, y * NC + core), along_z, along_x)),
        ((b1, b2, b3), ((z_pairs, z * NC + core), along_y, along_x)),
    )
    share = HID // 3
    def arrived(n, hop):
        boxes, route = plan[n]
        peers = route[hop][0]
        bulk(4 * n + hop, peers, boxes[hop].at[pl.ds(0, len(peers))]).wait_recv()

    for n, (boxes, route) in enumerate(plan):
        peers, mine = route[0]
        size = boxes[0].shape[1]
        columns = pl.ds(n * share, share)
        part = ppart[:, columns] + jnp.dot(pre, both[whole_q, columns], preferred_element_type=F32)
        for t in range(share // DIM):
            src[n * share + t * DIM:n * share + (t + 1) * DIM, :] = (
                part[:, t * DIM:(t + 1) * DIM].astype(BF16))
        start(4 * n, peers, lambda j: src.at[piece(n * share, size, j)], lambda j: boxes[0].at[j], mine)
        boxes[0][mine] = src[piece(n * share, size, mine), :]

    def hidden_tile(r):
        spot = pl.ds(r * CHUNK, CHUNK)
        rows = pre_t[:, whole_q].astype(F32).T.astype(BF16) if r == PR // CHUNK else ppre[spot, :]
        hidden_out_ref[spot, :] = nt_dot(rows, proj[...]).astype(BF16)

    def onward(n, hop):
        boxes, route = plan[n]
        peers, here = route[hop + 1]
        box = boxes[hop + 1]
        arrived(n, hop)
        box[here] = added(boxes[hop])
        start(4 * n + hop + 1, peers, lambda j: box.at[here], lambda j: box.at[j], here)

    def share_out(n):
        boxes, route = plan[n]
        peers, mine = route[0]
        size = boxes[0].shape[1]
        arrived(n, 2)
        gathered[piece(n * share, size, mine), :] = added(boxes[2])
        start(
            4 * n + 3, peers, lambda j: gathered.at[piece(n * share, size, mine)],
            lambda j: gathered.at[piece(n * share, size, j)], mine)

    loss = total - jnp.sum(onehot * score[0], axis=0, keepdims=True)
    for q in range(QN):
        loss_out[q] = jnp.sum(jnp.where(lane == q * QT, loss, 0.0))
    for hop in range(2):
        hidden_tile(2 * hop)
        hidden_tile(2 * hop + 1)
        for n in range(3):
            onward(n, hop)
    hidden_tile(4)
    hidden_tile(5)
    for n in (1, 2, 0):
        share_out(n)

    def spread(n):
        boxes, route = plan[n]
        peers = route[0][0]
        return bulk(4 * n + 3, peers, gathered.at[pl.ds(n * share, len(peers) * boxes[0].shape[1])])

    for n in range(3):
        spread(n).wait_recv()
    total_out[...] = gathered[...]

    for n, (boxes, route) in enumerate(plan):
        for hop in range(3):
            peers = route[hop][0]
            bulk(4 * n + hop, peers, boxes[hop].at[pl.ds(0, len(peers))]).wait_send()
        spread(n).wait_send()
    for b in (1, 2):
        send_query(b).wait_send()
        send_grad(b).wait_send()
    for n in range(4):
        send_lse(n).wait_send()


def run_step(query_lengths, passage_lengths, positives, query_hidden, passage_hidden, projection):
    dma = pltpu.SemaphoreType.DMA
    vmem = pl.BlockSpec(memory_space=pltpu.VMEM)
    hbm = pl.BlockSpec(memory_space=pltpu.HBM)
    vm = pltpu.VMEM
    ny = NYH * NYL
    share = HID // 3
    ya, za, xa = ny * NC, NZ * NC, NX * NC
    return pl.pallas_call(
        step_kernel,
        out_shape=(
            jax.ShapeDtypeStruct((QN,), F32),
            jax.ShapeDtypeStruct((PR + QR, HID), BF16),
            jax.ShapeDtypeStruct((HID, DIM), BF16),
        ),
        in_specs=[hbm] * 6,
        out_specs=(pl.BlockSpec(memory_space=pltpu.SMEM), vmem, vmem),
        scratch_shapes=[
            pltpu.SMEM((QN,), jnp.int32), pltpu.SMEM((PN,), jnp.int32), pltpu.SMEM((QN,), jnp.int32),
            vm((PR + QR, HID), BF16), vm((HID, DIM), BF16),
            vm((3, QR, QR), BF16), vm((DIM, QR), F32), vm((1, QR), F32),
            vm((PR, 2 * DIM), BF16), vm((DIM, PR), BF16), vm((PR, DIM), F32), vm((PR, 1), F32),
            vm((3, PR, QR), F32), vm((3, PR, QR), BF16),
            vm((3, TAIL, QR), F32), vm((3, TAIL, QR), F32), vm((3, TAIL, QR), F32),
            vm((3, TAIL, QR), F32), vm((TAIL, QR), F32), vm((QR, QR), BF16),
            vm((3, 8, QR), F32), vm((4, 8, QR), F32),
            vm((2, DIM, QR), BF16), vm((2, DIM, QR), BF16), vm((2, DIM, QR), BF16),
            vm((PR, DIM), BF16), vm((DIM, PR + QR), BF16),
            vm((PR, DIM), F32), vm((DIM, HID), F32),
            vm((HID, DIM), BF16),
            vm((ya, share // ya, DIM), BF16), vm((NZ, share // ya, DIM), BF16), vm((NX, share // ya, DIM), BF16),
            vm((za, share // za, DIM), BF16), vm((ny, share // za, DIM), BF16), vm((NX, share // za, DIM), BF16),
            vm((xa, share // xa, DIM), BF16), vm((ny, share // xa, DIM), BF16), vm((NZ, share // xa, DIM), BF16),
            vm((HID, DIM), BF16),
            dma((6,)), dma((2,)), dma((2,)), dma((4,)), dma((4,)), dma((2,)), dma((2,)),
            dma((12,)), dma((12,)),
        ],
        compiler_params=pltpu.CompilerParams(
            collective_id=0, has_side_effects=True, vmem_limit_bytes=24 * 1024 * 1024),
    )(query_lengths, passage_lengths, positives, query_hidden, passage_hidden, projection)


def finish_kernel(loss, hidden, total, loss_any, gq_any, gp_any, gproj_any, gproj, sem):
    puts = [
        pltpu.make_async_copy(near, far, sem.at[n])
        for n, (near, far) in enumerate((
            (hidden.at[pl.ds(0, PR)], gp_any), (hidden.at[pl.ds(PR, QR)], gq_any),
            (loss, loss_any), (gproj, gproj_any)))]
    for put in puts[:3]:
        put.start()
    for n in range(HID // DIM):
        spot = pl.ds(n * DIM, DIM)
        gproj[spot, :] = total[spot, :].astype(F32).T * (1.0 / (NB * NMP))
    puts[3].start()
    for put in puts:
        put.wait()


def run_finish(loss, hidden, total):
    vmem = pl.BlockSpec(memory_space=pltpu.VMEM)
    hbm = pl.BlockSpec(memory_space=pl.ANY)
    return pl.pallas_call(
        finish_kernel,
        out_shape=(
            jax.ShapeDtypeStruct((QN,), F32),
            jax.ShapeDtypeStruct((QR, HID), BF16),
            jax.ShapeDtypeStruct((PR, HID), BF16),
            jax.ShapeDtypeStruct((HID, DIM), F32),
        ),
        in_specs=[hbm, vmem, vmem],
        out_specs=(hbm, hbm, hbm, hbm),
        scratch_shapes=[pltpu.VMEM((HID, DIM), F32), pltpu.SemaphoreType.DMA((4,))],
        compiler_params=pltpu.CompilerParams(vmem_limit_bytes=16 * 1024 * 1024),
    )(loss, hidden, total)


def per_device(query_hidden, passage_hidden, projection, query_lengths, passage_lengths, positives):
    loss, hidden, total = run_step(*(
        pltpu.with_memory_space_constraint(v, pltpu.HBM) for v in (
            query_lengths, passage_lengths, positives, query_hidden, passage_hidden, projection)))
    return run_finish(loss, hidden, total)


def solution(mesh):
    in_specs = (
        P(("batch", "mp"), None),
        P(("batch", "mp"), None),
        P(),
        P(("batch", "mp")),
        P(("batch", "mp")),
        P(("batch", "mp")),
    )
    out_specs = (P(("batch", "mp")), P(("batch", "mp"), None), P(("batch", "mp"), None), P())
    return jax.shard_map(
        per_device, mesh=mesh, in_specs=in_specs, out_specs=out_specs, check_vma=False
    )
```

```python
import jax
import jax.numpy as jnp
from jax import lax
from jax.experimental import pallas as pl
from jax.experimental.pallas import tpu as pltpu
from jax.sharding import PartitionSpec as P

inner_scale = 128.0
outer_scale = 8.0
loss_scale = 32.0
norm_eps = 1e-06
hidden_out = -1e30

NX, NZ, NYH, NYL, NC = 4, 8, 4, 2, 2
NMP = NYL * NC
NB = NX * NZ * NYH
MESH = pl.DeviceIdType.MESH
F32 = jnp.float32
BF16 = jnp.bfloat16
QN, QT, PN, PT = 8, 32, 10, 128
QR, PR, DIM, HID = QN * QT, PN * PT, 128, 768
TAIL = 16
HOPS = (1, 2, -1, -2)
LSE_READY = (1, 0, 2, 2)
CHUNK = 256
UNROLL = 2


def exact_iota(shape, axis):
    return lax.broadcasted_iota(jnp.int32, shape, axis)


def nt_dot(left, right):
    return lax.dot_general(left, right, (((1,), (1,)), ((), ())), preferred_element_type=F32)


def log_sum(rows):
    top = jnp.maximum(jnp.maximum(rows[0], rows[1]), rows[2])
    return top + jnp.log(jnp.exp(rows[0] - top) + jnp.exp(rows[1] - top) + jnp.exp(rows[2] - top))


def turned(here, count):
    order = sorted(range(count), key=lambda a: -min(a, count - a))
    spots = []
    for a in order:
        there = here + a
        spots.append((a, jnp.where(there >= count, there - count, there) if a else here))
    return spots


def step_kernel(
    qlen_any, plen_any, pos_any, qh_any, ph_any, proj_any,
    loss_out, hidden_out_ref, total_out,
    qlen, plen, pos, both, proj, qbuf, qunit, qrad, paug, ptr, punit, prad, power, gsim,
    tops, tots, score, keeps, coef, member, lse_own, lse_in, tq_out, tq_in, qscaled,
    ppre, pre_t, pgrad, ppart, src, a1, a2, a3, b1, b2, b3, c1, c2, c3, gathered,
    in_sem, qs, qr, ls, lr, ts, tr, push, pull,
):
    bi = lax.axis_index("batch")
    mi = lax.axis_index("mp")
    yh = lax.rem(bi, NYH)
    up = lax.div(bi, NYH)
    z = lax.rem(up, NZ)
    x = lax.div(up, NZ)
    yl = lax.div(mi, NC)
    core = lax.rem(mi, NC)
    y = yh * NYL + yl
    xz = bi - yh

    cores = turned(core, NC)

    def at_y(spot, side):
        return (xz + lax.div(spot, NYL), lax.rem(spot, NYL) * NC + side)

    def at_z(spot, side):
        return (bi + (spot - z) * NYH, mi + (side - core))

    def at_x(spot, side):
        return (bi + (spot - x) * (NYH * NZ), mi + (side - core))

    def pairs(here, count, place):
        return [
            (spot * NC + side, place(spot, side))
            for a, spot in turned(here, count) for c, side in cores if a or c]

    def line(here, count, place):
        return [(spot, place(spot, core)) for a, spot in turned(here, count) if a]

    def ring_peer(hop):
        there = bi + hop
        there = jnp.where(there >= NB, there - NB, there) if hop > 0 else jnp.where(there < 0, there + NB, there)
        return (there, mi)

    ring = {hop: ring_peer(hop) for hop in HOPS}

    whole_p, whole_q = pl.ds(0, PR), pl.ds(PR, QR)
    get_proj = pltpu.make_async_copy(proj_any, proj, in_sem.at[0])
    get_qh = pltpu.make_async_copy(qh_any, both.at[whole_q], in_sem.at[1])
    get_ph = pltpu.make_async_copy(ph_any, both.at[whole_p], in_sem.at[2])

    small = [
        pltpu.make_async_copy(far, near, in_sem.at[3 + n])
        for n, (far, near) in enumerate(((qlen_any, qlen), (plen_any, plen), (pos_any, pos)))]

    @pl.when(bi >= 0)
    def _():
        for copy in small:
            copy.start()
        get_proj.start()
        get_qh.start()
        get_ph.start()

    barrier = pltpu.get_barrier_semaphore()

    def greet(places):
        for where in places:
            pl.semaphore_signal(barrier, inc=1, device_id=where, device_id_type=MESH)
        return len(places)

    greeted = greet([ring[hop] for hop in HOPS])
    x_pairs = pairs(x, NX, at_x)
    y_line = line(y, NYH * NYL, at_y)
    z_line = line(z, NZ, at_z)
    greeted += greet([where for _, where in y_line + z_line + x_pairs])

    for copy in small:
        copy.wait()
    lane = exact_iota((1, QR), 1)
    keep = jnp.zeros((1, QR), F32)
    for q in range(QN):
        token = lane - q * QT
        keep = jnp.where((token >= 0) & (token < qlen[q]), 1.0, keep)
    tail_row = exact_iota((TAIL, QR), 0)
    qbuf[0, DIM:DIM + TAIL, :] = jnp.where(
        tail_row == 0, 1.0, jnp.where(tail_row == 1, keep, 0.0)).astype(BF16)
    for b in range(3):
        qbuf[b, DIM + TAIL:, :] = jnp.zeros((QR - DIM - TAIL, QR), BF16)

    get_proj.wait()
    get_qh.wait()
    before = jnp.dot(both[whole_q, :], proj[...], preferred_element_type=F32).T
    radius = jnp.sqrt(jnp.sum(before * before, axis=0, keepdims=True) + norm_eps)
    inverse = 1.0 / radius
    unit = before * inverse
    qunit[...] = unit
    qrad[...] = inverse
    qbuf[0, :DIM, :] = unit.astype(BF16)

    pl.semaphore_wait(barrier, greeted)

    def send_query(b):
        part = pl.ds(0, DIM + TAIL)
        return pltpu.make_async_remote_copy(
            src_ref=qbuf.at[0, part], dst_ref=qbuf.at[b, part], send_sem=qs.at[b - 1],
            recv_sem=qr.at[b - 1], device_id=ring[b], device_id_type=MESH)

    send_query(2).start()
    send_query(1).start()

    member[...] = jnp.where(
        exact_iota((QR, QR), 0) // QT == exact_iota((QR, QR), 1) // QT, 1.0, 0.0).astype(BF16)
    tops[...] = jnp.zeros(tops.shape, F32)
    tots[...] = jnp.ones(tots.shape, F32)

    @pl.loop(0, PN)
    def _(c):
        spot = pl.ds(pl.multiple_of(c * PT, PT), PT)
        outside = (exact_iota((PT, DIM), 0) >= plen[c]) & (exact_iota((PT, DIM), 1) == 0)
        paug[spot, DIM:] = jnp.where(outside, hidden_out, 0.0).astype(BF16)

    get_ph.wait()

    for r in range(PR // CHUNK):
        spot = pl.ds(r * CHUNK, CHUNK)
        before = jnp.dot(both[spot, :], proj[...], preferred_element_type=F32)
        radius = jnp.sqrt(jnp.sum(before * before, axis=-1, keepdims=True) + norm_eps)
        inverse = 1.0 / radius
        unit = before * inverse
        punit[spot, :] = unit
        prad[spot, :] = inverse
        embed = unit.astype(BF16)
        paug[spot, :DIM] = embed * jnp.array(inner_scale, BF16)
        ptr[:, spot] = embed.astype(F32).T.astype(BF16)

    def forward(b):
        power[b] = jnp.dot(paug[...], qbuf[b], preferred_element_type=F32)

        @pl.loop(0, PN // UNROLL)
        def _(step):
            for k in range(UNROLL):
                c = step * UNROLL + k
                spot = pl.ds(pl.multiple_of(c * PT, PT), PT)
                logits = power[b, spot, :]
                top = jnp.max(logits, axis=0, keepdims=True)
                powers = jnp.exp(logits - top)
                power[b, spot, :] = powers
                tops[b, pl.ds(c, 1), :] = top
                tots[b, pl.ds(c, 1), :] = jnp.sum(powers, axis=0, keepdims=True)

        kept = qbuf[b, DIM:DIM + TAIL, :].astype(F32)[1:2, :]
        keeps[b] = jnp.broadcast_to(kept, (TAIL, QR))
        best = (jnp.log(tots[b]) + tops[b]) * (1.0 / inner_scale) * kept
        high = best.astype(BF16)
        rest = best - high.astype(F32)
        middle = rest.astype(BF16)
        low = (rest - middle.astype(F32)).astype(BF16)
        sums = jnp.dot(
            jnp.concatenate([high, middle, low], axis=0), member[...], preferred_element_type=F32)
        scores = outer_scale * (sums[:TAIL] + (sums[TAIL:2 * TAIL] + sums[2 * TAIL:]))
        scores = jnp.where(exact_iota((TAIL, QR), 0) < PN, scores, hidden_out)
        score[b] = scores
        top = jnp.max(scores, axis=0, keepdims=True)
        total = top + jnp.log(jnp.sum(jnp.exp(scores - top), axis=0, keepdims=True))
        for k in range(b, 3):
            lse_own[k, b:b + 1, :] = total

    def to_grads(b, dscore):
        coef[...] = dscore * keeps[b] * (outer_scale * loss_scale) / tots[b]

        @pl.loop(0, PN // UNROLL)
        def _(step):
            for k in range(UNROLL):
                c = step * UNROLL + k
                spot = pl.ds(pl.multiple_of(c * PT, PT), PT)
                gsim[b, spot, :] = (power[b, spot, :] * coef[pl.ds(c, 1), :]).astype(BF16)

    def send_grad(b):
        return pltpu.make_async_remote_copy(
            src_ref=tq_out.at[b - 1], dst_ref=tq_in.at[b - 1], send_sem=ts.at[b - 1],
            recv_sem=tr.at[b - 1], device_id=ring[-b], device_id_type=MESH)

    def send_lse(n):
        return pltpu.make_async_remote_copy(
            src_ref=lse_own.at[LSE_READY[n]], dst_ref=lse_in.at[n], send_sem=ls.at[n], recv_sem=lr.at[n],
            device_id=ring[HOPS[n]], device_id_type=MESH)

    lse_own[...] = jnp.zeros(lse_own.shape, F32)
    for b in range(3):
        if b:
            send_query(b).wait_recv()
        forward(b)
        for n in range(4):
            if LSE_READY[n] == b:
                send_lse(n).start()
    for b in (2, 1):
        to_grads(b, jnp.exp(score[b] - lse_own[2, b:b + 1, :]))
        tq_out[b - 1] = jnp.dot(ptr[...], gsim[b], preferred_element_type=F32).astype(BF16)
        send_grad(b).start()

    place = jnp.zeros((1, QR), jnp.int32)
    for q in range(QN):
        place = jnp.where(lane // QT == q, pos[q], place)
    onehot = jnp.where(exact_iota((TAIL, QR), 0) == place, 1.0, 0.0)

    def scaled(b, rows):
        factor = jnp.exp(lse_own[2, b:b + 1, :] - log_sum(rows))
        qscaled[b - 1] = (qbuf[b, :DIM, :].astype(F32) * factor).astype(BF16)

    send_lse(0).wait_recv()
    send_lse(1).wait_recv()
    scaled(2, (lse_in[1, 0:1, :], lse_in[0, 1:2, :], lse_own[2, 2:3, :]))
    pgrad[...] = nt_dot(gsim[2], qscaled[1])
    send_lse(2).wait_recv()
    scaled(1, (lse_in[0, 0:1, :], lse_own[2, 1:2, :], lse_in[2, 2:3, :]))
    pgrad[...] += nt_dot(gsim[1], qscaled[0])
    send_lse(3).wait_recv()
    total = log_sum((lse_own[2, 0:1, :], lse_in[2, 1:2, :], lse_in[3, 2:3, :]))
    to_grads(0, jnp.exp(score[0] - total) - onehot)

    for r in range(PR // CHUNK):
        spot = pl.ds(r * CHUNK, CHUNK)
        grad = pgrad[spot, :] + nt_dot(gsim[0, spot, :], qbuf[0, :DIM, :])
        unit = punit[spot, :]
        pre = (grad - unit * jnp.sum(unit * grad, axis=-1, keepdims=True)) * prad[spot, :]
        pre = pre.astype(BF16)
        ppre[spot, :] = pre
        pre_t[:, spot] = pre.astype(F32).T.astype(BF16)

    ppart[...] = jnp.dot(pre_t[:, whole_p], both[whole_p, :], preferred_element_type=F32)
    qgrad = jnp.dot(ptr[...], gsim[0], preferred_element_type=F32)

    send_grad(1).wait_recv()
    send_grad(2).wait_recv()
    qgrad += jnp.exp(lse_in[2, 1:2, :] - total) * tq_in[0].astype(F32)
    qgrad += jnp.exp(lse_in[3, 2:3, :] - total) * tq_in[1].astype(F32)
    unit = qunit[...]
    pre = (qgrad - unit * jnp.sum(unit * qgrad, axis=0, keepdims=True)) * qrad[...]
    pre = pre.astype(BF16)
    pre_t[:, whole_q] = pre

    def piece(first, size, j):
        return pl.ds(pl.multiple_of(first + j * size, size), size)

    def start(stage, peers, source, target, mine):
        for j, where in peers:
            pltpu.make_async_remote_copy(
                src_ref=source(j), dst_ref=target(mine), send_sem=push.at[stage],
                recv_sem=pull.at[stage], device_id=where, device_id_type=MESH).start()

    def bulk(stage, peers, whole):
        return pltpu.make_async_remote_copy(
            src_ref=whole, dst_ref=whole, send_sem=push.at[stage], recv_sem=pull.at[stage],
            device_id=peers[0][1], device_id_type=MESH)

    def added(box):
        return jnp.sum(box[...].astype(F32), axis=0).astype(BF16)

    along_y, along_z, around_x = (y_line, y), (z_line, z), (x_pairs, x * NC + core)
    plan = (
        ((c1, c2, c3), (around_x, along_y, along_z)),
        ((a1, a2, a3), (along_y, along_z, around_x)),
        ((b1, b2, b3), (along_z, along_y, around_x)),
    )
    share = HID // 3
    def arrived(n, hop):
        boxes, route = plan[n]
        peers = route[hop][0]
        bulk(4 * n + hop, peers, boxes[hop].at[pl.ds(0, len(peers))]).wait_recv()

    for n, (boxes, route) in enumerate(plan):
        peers, mine = route[0]
        size = boxes[0].shape[1]
        columns = pl.ds(n * share, share)
        part = ppart[:, columns] + jnp.dot(pre, both[whole_q, columns], preferred_element_type=F32)
        for t in range(share // DIM):
            src[n * share + t * DIM:n * share + (t + 1) * DIM, :] = (
                part[:, t * DIM:(t + 1) * DIM].astype(BF16))
        start(4 * n, peers, lambda j: src.at[piece(n * share, size, j)], lambda j: boxes[0].at[j], mine)
        boxes[0][mine] = src[piece(n * share, size, mine), :]

    def hidden_tile(r):
        spot = pl.ds(r * CHUNK, CHUNK)
        rows = pre_t[:, whole_q].astype(F32).T.astype(BF16) if r == PR // CHUNK else ppre[spot, :]
        hidden_out_ref[spot, :] = nt_dot(rows, proj[...]).astype(BF16)

    def onward(n, hop):
        boxes, route = plan[n]
        peers, here = route[hop + 1]
        box = boxes[hop + 1]
        arrived(n, hop)
        box[here] = added(boxes[hop])
        start(4 * n + hop + 1, peers, lambda j: box.at[here], lambda j: box.at[j], here)

    def share_out(n):
        boxes, route = plan[n]
        peers, mine = route[0]
        size = boxes[0].shape[1]
        arrived(n, 2)
        gathered[piece(n * share, size, mine), :] = added(boxes[2])
        start(
            4 * n + 3, peers, lambda j: gathered.at[piece(n * share, size, mine)],
            lambda j: gathered.at[piece(n * share, size, j)], mine)

    loss = total - jnp.sum(onehot * score[0], axis=0, keepdims=True)
    for q in range(QN):
        loss_out[q] = jnp.sum(jnp.where(lane == q * QT, loss, 0.0))
    for hop in range(2):
        hidden_tile(2 * hop)
        hidden_tile(2 * hop + 1)
        for n in range(3):
            onward(n, hop)
    hidden_tile(4)
    hidden_tile(5)
    for n in (1, 2, 0):
        share_out(n)

    def spread(n):
        boxes, route = plan[n]
        peers = route[0][0]
        return bulk(4 * n + 3, peers, gathered.at[pl.ds(n * share, len(peers) * boxes[0].shape[1])])

    for n in range(3):
        spread(n).wait_recv()
    total_out[...] = gathered[...]

    for n, (boxes, route) in enumerate(plan):
        for hop in range(3):
            peers = route[hop][0]
            bulk(4 * n + hop, peers, boxes[hop].at[pl.ds(0, len(peers))]).wait_send()
        spread(n).wait_send()
    for b in (1, 2):
        send_query(b).wait_send()
        send_grad(b).wait_send()
    for n in range(4):
        send_lse(n).wait_send()


def run_step(query_lengths, passage_lengths, positives, query_hidden, passage_hidden, projection):
    dma = pltpu.SemaphoreType.DMA
    vmem = pl.BlockSpec(memory_space=pltpu.VMEM)
    hbm = pl.BlockSpec(memory_space=pltpu.HBM)
    vm = pltpu.VMEM
    ny = NYH * NYL
    share = HID // 3
    xa = NX * NC
    return pl.pallas_call(
        step_kernel,
        out_shape=(
            jax.ShapeDtypeStruct((QN,), F32),
            jax.ShapeDtypeStruct((PR + QR, HID), BF16),
            jax.ShapeDtypeStruct((HID, DIM), BF16),
        ),
        in_specs=[hbm] * 6,
        out_specs=(pl.BlockSpec(memory_space=pltpu.SMEM), vmem, vmem),
        scratch_shapes=[
            pltpu.SMEM((QN,), jnp.int32), pltpu.SMEM((PN,), jnp.int32), pltpu.SMEM((QN,), jnp.int32),
            vm((PR + QR, HID), BF16), vm((HID, DIM), BF16),
            vm((3, QR, QR), BF16), vm((DIM, QR), F32), vm((1, QR), F32),
            vm((PR, 2 * DIM), BF16), vm((DIM, PR), BF16), vm((PR, DIM), F32), vm((PR, 1), F32),
            vm((3, PR, QR), F32), vm((3, PR, QR), BF16),
            vm((3, TAIL, QR), F32), vm((3, TAIL, QR), F32), vm((3, TAIL, QR), F32),
            vm((3, TAIL, QR), F32), vm((TAIL, QR), F32), vm((QR, QR), BF16),
            vm((3, 8, QR), F32), vm((4, 8, QR), F32),
            vm((2, DIM, QR), BF16), vm((2, DIM, QR), BF16), vm((2, DIM, QR), BF16),
            vm((PR, DIM), BF16), vm((DIM, PR + QR), BF16),
            vm((PR, DIM), F32), vm((DIM, HID), F32),
            vm((HID, DIM), BF16),
            vm((ny, share // ny, DIM), BF16), vm((NZ, share // ny, DIM), BF16), vm((xa, share // ny, DIM), BF16),
            vm((NZ, share // NZ, DIM), BF16), vm((ny, share // NZ, DIM), BF16), vm((xa, share // NZ, DIM), BF16),
            vm((xa, share // xa, DIM), BF16), vm((ny, share // xa, DIM), BF16), vm((NZ, share // xa, DIM), BF16),
            vm((HID, DIM), BF16),
            dma((6,)), dma((2,)), dma((2,)), dma((4,)), dma((4,)), dma((2,)), dma((2,)),
            dma((12,)), dma((12,)),
        ],
        compiler_params=pltpu.CompilerParams(
            collective_id=0, has_side_effects=True, vmem_limit_bytes=24 * 1024 * 1024),
    )(query_lengths, passage_lengths, positives, query_hidden, passage_hidden, projection)


def finish_kernel(loss, hidden, total, loss_any, gq_any, gp_any, gproj_any, gproj, sem):
    puts = [
        pltpu.make_async_copy(near, far, sem.at[n])
        for n, (near, far) in enumerate((
            (hidden.at[pl.ds(0, PR)], gp_any), (hidden.at[pl.ds(PR, QR)], gq_any),
            (loss, loss_any), (gproj, gproj_any)))]
    for put in puts[:3]:
        put.start()
    for n in range(HID // DIM):
        spot = pl.ds(n * DIM, DIM)
        gproj[spot, :] = total[spot, :].astype(F32).T * (1.0 / (NB * NMP))
    puts[3].start()
    for put in puts:
        put.wait()


def run_finish(loss, hidden, total):
    vmem = pl.BlockSpec(memory_space=pltpu.VMEM)
    hbm = pl.BlockSpec(memory_space=pl.ANY)
    return pl.pallas_call(
        finish_kernel,
        out_shape=(
            jax.ShapeDtypeStruct((QN,), F32),
            jax.ShapeDtypeStruct((QR, HID), BF16),
            jax.ShapeDtypeStruct((PR, HID), BF16),
            jax.ShapeDtypeStruct((HID, DIM), F32),
        ),
        in_specs=[hbm, vmem, vmem],
        out_specs=(hbm, hbm, hbm, hbm),
        scratch_shapes=[pltpu.VMEM((HID, DIM), F32), pltpu.SemaphoreType.DMA((4,))],
        compiler_params=pltpu.CompilerParams(vmem_limit_bytes=16 * 1024 * 1024),
    )(loss, hidden, total)


def per_device(query_hidden, passage_hidden, projection, query_lengths, passage_lengths, positives):
    loss, hidden, total = run_step(*(
        pltpu.with_memory_space_constraint(v, pltpu.HBM) for v in (
            query_lengths, passage_lengths, positives, query_hidden, passage_hidden, projection)))
    return run_finish(loss, hidden, total)


def solution(mesh):
    in_specs = (
        P(("batch", "mp"), None),
        P(("batch", "mp"), None),
        P(),
        P(("batch", "mp")),
        P(("batch", "mp")),
        P(("batch", "mp")),
    )
    out_specs = (P(("batch", "mp")), P(("batch", "mp"), None), P(("batch", "mp"), None), P())
    return jax.shard_map(
        per_device, mesh=mesh, in_specs=in_specs, out_specs=out_specs, check_vma=False
    )
```

```python
import jax
import jax.numpy as jnp
from jax import lax
from jax.experimental import pallas as pl
from jax.experimental.pallas import tpu as pltpu
from jax.sharding import PartitionSpec as P

inner_scale = 128.0
outer_scale = 8.0
loss_scale = 32.0
norm_eps = 1e-06
hidden_out = -1e30

NX, NZ, NYH, NYL, NC = 4, 8, 4, 2, 2
NMP = NYL * NC
NB = NX * NZ * NYH
MESH = pl.DeviceIdType.MESH
F32 = jnp.float32
BF16 = jnp.bfloat16
QN, QT, PN, PT = 8, 32, 10, 128
QR, PR, DIM, HID = QN * QT, PN * PT, 128, 768
TAIL = 16
HOPS = (1, 2, -1, -2)
LSE_READY = (1, 0, 2, 2)
CHUNK = 256
ROWS = 256
UNROLL = 2


def exact_iota(shape, axis):
    return lax.broadcasted_iota(jnp.int32, shape, axis)


def nt_dot(left, right):
    return lax.dot_general(left, right, (((1,), (1,)), ((), ())), preferred_element_type=F32)


def log_sum(rows):
    top = jnp.maximum(jnp.maximum(rows[0], rows[1]), rows[2])
    return top + jnp.log(jnp.exp(rows[0] - top) + jnp.exp(rows[1] - top) + jnp.exp(rows[2] - top))


def turned(here, count):
    order = sorted(range(count), key=lambda a: -min(a, count - a))
    spots = []
    for a in order:
        there = here + a
        spots.append((a, jnp.where(there >= count, there - count, there) if a else here))
    return spots


def step_kernel(
    qlen_any, plen_any, pos_any, qh_any, ph_any, proj_any,
    loss_out, hidden_out_ref, total_out,
    qlen, plen, pos, both, proj, qbuf, qunit, qrad, paug, ptr, punit, prad, power, gsim,
    tops, tots, score, keeps, coef, member, lse_own, lse_in, tq_out, tq_in, qscaled,
    ppre, pre_t, pgrad, ppart, src, a1, a2, a3, b1, b2, b3, c1, c2, c3, gathered,
    in_sem, qs, qr, ls, lr, ts, tr, push, pull,
):
    bi = lax.axis_index("batch")
    mi = lax.axis_index("mp")
    yh = lax.rem(bi, NYH)
    up = lax.div(bi, NYH)
    z = lax.rem(up, NZ)
    x = lax.div(up, NZ)
    yl = lax.div(mi, NC)
    core = lax.rem(mi, NC)
    y = yh * NYL + yl
    xz = bi - yh

    cores = turned(core, NC)

    def at_y(spot, side):
        return (xz + lax.div(spot, NYL), lax.rem(spot, NYL) * NC + side)

    def at_z(spot, side):
        return (bi + (spot - z) * NYH, mi + (side - core))

    def at_x(spot, side):
        return (bi + (spot - x) * (NYH * NZ), mi + (side - core))

    def pairs(here, count, place):
        return [
            (spot * NC + side, place(spot, side))
            for a, spot in turned(here, count) for c, side in cores if a or c]

    def line(here, count, place):
        return [(spot, place(spot, core)) for a, spot in turned(here, count) if a]

    def ring_peer(hop):
        there = bi + hop
        there = jnp.where(there >= NB, there - NB, there) if hop > 0 else jnp.where(there < 0, there + NB, there)
        return (there, mi)

    ring = {hop: ring_peer(hop) for hop in HOPS}

    whole_p, whole_q = pl.ds(0, PR), pl.ds(PR, QR)
    get_proj = pltpu.make_async_copy(proj_any, proj, in_sem.at[0])
    get_qh = pltpu.make_async_copy(qh_any, both.at[whole_q], in_sem.at[1])
    get_ph = pltpu.make_async_copy(ph_any, both.at[whole_p], in_sem.at[2])

    small = [
        pltpu.make_async_copy(far, near, in_sem.at[3 + n])
        for n, (far, near) in enumerate(((qlen_any, qlen), (plen_any, plen), (pos_any, pos)))]

    @pl.when(bi >= 0)
    def _():
        for copy in small:
            copy.start()
        get_proj.start()
        get_qh.start()
        get_ph.start()

    barrier = pltpu.get_barrier_semaphore()

    def greet(places):
        for where in places:
            pl.semaphore_signal(barrier, inc=1, device_id=where, device_id_type=MESH)
        return len(places)

    greeted = greet([ring[hop] for hop in HOPS])
    x_pairs = pairs(x, NX, at_x)
    y_line = line(y, NYH * NYL, at_y)
    z_line = line(z, NZ, at_z)
    greeted += greet([where for _, where in y_line + z_line + x_pairs])

    for copy in small:
        copy.wait()
    lane = exact_iota((1, QR), 1)
    keep = jnp.zeros((1, QR), F32)
    for q in range(QN):
        token = lane - q * QT
        keep = jnp.where((token >= 0) & (token < qlen[q]), 1.0, keep)
    tail_row = exact_iota((TAIL, QR), 0)
    qbuf[0, DIM:DIM + TAIL, :] = jnp.where(
        tail_row == 0, 1.0, jnp.where(tail_row == 1, keep, 0.0)).astype(BF16)
    for b in range(3):
        qbuf[b, DIM + TAIL:, :] = jnp.zeros((QR - DIM - TAIL, QR), BF16)

    get_proj.wait()
    get_qh.wait()
    before = jnp.dot(both[whole_q, :], proj[...], preferred_element_type=F32).T
    radius = jnp.sqrt(jnp.sum(before * before, axis=0, keepdims=True) + norm_eps)
    inverse = 1.0 / radius
    unit = before * inverse
    qunit[...] = unit
    qrad[...] = inverse
    qbuf[0, :DIM, :] = unit.astype(BF16)

    pl.semaphore_wait(barrier, greeted)

    def send_query(b):
        part = pl.ds(0, DIM + TAIL)
        return pltpu.make_async_remote_copy(
            src_ref=qbuf.at[0, part], dst_ref=qbuf.at[b, part], send_sem=qs.at[b - 1],
            recv_sem=qr.at[b - 1], device_id=ring[b], device_id_type=MESH)

    send_query(2).start()
    send_query(1).start()

    member[...] = jnp.where(
        exact_iota((QR, QR), 0) // QT == exact_iota((QR, QR), 1) // QT, 1.0, 0.0).astype(BF16)
    tops[...] = jnp.zeros(tops.shape, F32)
    tots[...] = jnp.ones(tots.shape, F32)

    @pl.loop(0, PN)
    def _(c):
        spot = pl.ds(pl.multiple_of(c * PT, PT), PT)
        outside = (exact_iota((PT, DIM), 0) >= plen[c]) & (exact_iota((PT, DIM), 1) == 0)
        paug[spot, DIM:] = jnp.where(outside, hidden_out, 0.0).astype(BF16)

    get_ph.wait()

    for r in range(PR // ROWS):
        spot = pl.ds(r * ROWS, ROWS)
        before = jnp.dot(both[spot, :], proj[...], preferred_element_type=F32)
        radius = jnp.sqrt(jnp.sum(before * before, axis=-1, keepdims=True) + norm_eps)
        inverse = 1.0 / radius
        unit = before * inverse
        punit[spot, :] = unit
        prad[spot, :] = inverse
        embed = unit.astype(BF16)
        paug[spot, :DIM] = embed * jnp.array(inner_scale, BF16)
        ptr[:, spot] = embed.T

    def forward(b):
        power[b] = jnp.dot(paug[...], qbuf[b], preferred_element_type=F32)

        @pl.loop(0, PN // UNROLL)
        def _(step):
            for k in range(UNROLL):
                c = step * UNROLL + k
                spot = pl.ds(pl.multiple_of(c * PT, PT), PT)
                logits = power[b, spot, :]
                top = jnp.max(logits, axis=0, keepdims=True)
                powers = jnp.exp(logits - top)
                power[b, spot, :] = powers
                tops[b, pl.ds(c, 1), :] = top
                tots[b, pl.ds(c, 1), :] = jnp.sum(powers, axis=0, keepdims=True)

        kept = qbuf[b, DIM:DIM + TAIL, :].astype(F32)[1:2, :]
        keeps[b] = jnp.broadcast_to(kept, (TAIL, QR))
        best = (jnp.log(tots[b]) + tops[b]) * (1.0 / inner_scale) * kept
        high = best.astype(BF16)
        rest = best - high.astype(F32)
        middle = rest.astype(BF16)
        low = (rest - middle.astype(F32)).astype(BF16)
        sums = jnp.dot(
            jnp.concatenate([high, middle, low], axis=0), member[...], preferred_element_type=F32)
        scores = outer_scale * (sums[:TAIL] + (sums[TAIL:2 * TAIL] + sums[2 * TAIL:]))
        scores = jnp.where(exact_iota((TAIL, QR), 0) < PN, scores, hidden_out)
        score[b] = scores
        top = jnp.max(scores, axis=0, keepdims=True)
        total = top + jnp.log(jnp.sum(jnp.exp(scores - top), axis=0, keepdims=True))
        for k in range(b, 3):
            lse_own[k, b:b + 1, :] = total

    def to_grads(b, dscore):
        coef[...] = dscore * keeps[b] * (outer_scale * loss_scale) / tots[b]

        @pl.loop(0, PN // UNROLL)
        def _(step):
            for k in range(UNROLL):
                c = step * UNROLL + k
                spot = pl.ds(pl.multiple_of(c * PT, PT), PT)
                gsim[b, spot, :] = (power[b, spot, :] * coef[pl.ds(c, 1), :]).astype(BF16)

    def send_grad(b):
        return pltpu.make_async_remote_copy(
            src_ref=tq_out.at[b - 1], dst_ref=tq_in.at[b - 1], send_sem=ts.at[b - 1],
            recv_sem=tr.at[b - 1], device_id=ring[-b], device_id_type=MESH)

    def send_lse(n):
        return pltpu.make_async_remote_copy(
            src_ref=lse_own.at[LSE_READY[n]], dst_ref=lse_in.at[n], send_sem=ls.at[n], recv_sem=lr.at[n],
            device_id=ring[HOPS[n]], device_id_type=MESH)

    lse_own[...] = jnp.zeros(lse_own.shape, F32)
    for b in range(3):
        if b:
            send_query(b).wait_recv()
        forward(b)
        for n in range(4):
            if LSE_READY[n] == b:
                send_lse(n).start()
    for b in (2, 1):
        to_grads(b, jnp.exp(score[b] - lse_own[2, b:b + 1, :]))
        tq_out[b - 1] = jnp.dot(ptr[...], gsim[b], preferred_element_type=F32).astype(BF16)
        send_grad(b).start()

    place = jnp.zeros((1, QR), jnp.int32)
    for q in range(QN):
        place = jnp.where(lane // QT == q, pos[q], place)
    onehot = jnp.where(exact_iota((TAIL, QR), 0) == place, 1.0, 0.0)

    def scaled(b, rows):
        factor = jnp.exp(lse_own[2, b:b + 1, :] - log_sum(rows))
        qscaled[b - 1] = (qbuf[b, :DIM, :].astype(F32) * factor).astype(BF16)

    send_lse(0).wait_recv()
    send_lse(1).wait_recv()
    scaled(2, (lse_in[1, 0:1, :], lse_in[0, 1:2, :], lse_own[2, 2:3, :]))
    pgrad[...] = nt_dot(gsim[2], qscaled[1])
    send_lse(2).wait_recv()
    scaled(1, (lse_in[0, 0:1, :], lse_own[2, 1:2, :], lse_in[2, 2:3, :]))
    pgrad[...] += nt_dot(gsim[1], qscaled[0])
    send_lse(3).wait_recv()
    total = log_sum((lse_own[2, 0:1, :], lse_in[2, 1:2, :], lse_in[3, 2:3, :]))
    to_grads(0, jnp.exp(score[0] - total) - onehot)

    for r in range(PR // ROWS):
        spot = pl.ds(r * ROWS, ROWS)
        grad = pgrad[spot, :] + nt_dot(gsim[0, spot, :], qbuf[0, :DIM, :])
        unit = punit[spot, :]
        pre = (grad - unit * jnp.sum(unit * grad, axis=-1, keepdims=True)) * prad[spot, :]
        pre = pre.astype(BF16)
        ppre[spot, :] = pre
        pre_t[:, spot] = pre.T

    ppart[...] = jnp.dot(pre_t[:, whole_p], both[whole_p, :], preferred_element_type=F32)
    qgrad = jnp.dot(ptr[...], gsim[0], preferred_element_type=F32)

    send_grad(1).wait_recv()
    send_grad(2).wait_recv()
    qgrad += jnp.exp(lse_in[2, 1:2, :] - total) * tq_in[0].astype(F32)
    qgrad += jnp.exp(lse_in[3, 2:3, :] - total) * tq_in[1].astype(F32)
    unit = qunit[...]
    pre = (qgrad - unit * jnp.sum(unit * qgrad, axis=0, keepdims=True)) * qrad[...]
    pre = pre.astype(BF16)
    pre_t[:, whole_q] = pre

    def piece(first, size, j):
        return pl.ds(pl.multiple_of(first + j * size, size), size)

    def start(stage, peers, source, target, mine):
        for j, where in peers:
            pltpu.make_async_remote_copy(
                src_ref=source(j), dst_ref=target(mine), send_sem=push.at[stage],
                recv_sem=pull.at[stage], device_id=where, device_id_type=MESH).start()

    def bulk(stage, peers, whole):
        return pltpu.make_async_remote_copy(
            src_ref=whole, dst_ref=whole, send_sem=push.at[stage], recv_sem=pull.at[stage],
            device_id=peers[0][1], device_id_type=MESH)

    def added(box):
        return jnp.sum(box[...].astype(F32), axis=0).astype(BF16)

    along_y, along_z, around_x = (y_line, y), (z_line, z), (x_pairs, x * NC + core)
    plan = (
        ((a1, a2, a3), (along_y, along_z, around_x)),
        ((b1, b2, b3), (along_z, along_y, around_x)),
        ((c1, c2, c3), (around_x, along_y, along_z)),
    )
    share = HID // 3
    def arrived(n, hop):
        boxes, route = plan[n]
        peers = route[hop][0]
        bulk(4 * n + hop, peers, boxes[hop].at[pl.ds(0, len(peers))]).wait_recv()

    for n, (boxes, route) in enumerate(plan):
        peers, mine = route[0]
        size = boxes[0].shape[1]
        columns = pl.ds(n * share, share)
        part = ppart[:, columns] + jnp.dot(pre, both[whole_q, columns], preferred_element_type=F32)
        for t in range(share // DIM):
            src[n * share + t * DIM:n * share + (t + 1) * DIM, :] = (
                part[:, t * DIM:(t + 1) * DIM].astype(BF16))
        start(4 * n, peers, lambda j: src.at[piece(n * share, size, j)], lambda j: boxes[0].at[j], mine)
        boxes[0][mine] = src[piece(n * share, size, mine), :]

    def hidden_tile(r):
        spot = pl.ds(r * CHUNK, CHUNK)
        rows = pre_t[:, whole_q].astype(F32).T.astype(BF16) if r == PR // CHUNK else ppre[spot, :]
        hidden_out_ref[spot, :] = nt_dot(rows, proj[...]).astype(BF16)

    def onward(n, hop):
        boxes, route = plan[n]
        peers, here = route[hop + 1]
        box = boxes[hop + 1]
        arrived(n, hop)
        box[here] = added(boxes[hop])
        start(4 * n + hop + 1, peers, lambda j: box.at[here], lambda j: box.at[j], here)

    def share_out(n):
        boxes, route = plan[n]
        peers, mine = route[0]
        size = boxes[0].shape[1]
        arrived(n, 2)
        gathered[piece(n * share, size, mine), :] = added(boxes[2])
        start(
            4 * n + 3, peers, lambda j: gathered.at[piece(n * share, size, mine)],
            lambda j: gathered.at[piece(n * share, size, j)], mine)

    loss = total - jnp.sum(onehot * score[0], axis=0, keepdims=True)
    for q in range(QN):
        loss_out[q] = jnp.sum(jnp.where(lane == q * QT, loss, 0.0))
    for hop in range(2):
        hidden_tile(2 * hop)
        hidden_tile(2 * hop + 1)
        for n in (2, 0, 1):
            onward(n, hop)
    hidden_tile(4)
    hidden_tile(5)
    for n in (0, 1, 2):
        share_out(n)

    def spread(n):
        boxes, route = plan[n]
        peers = route[0][0]
        return bulk(4 * n + 3, peers, gathered.at[pl.ds(n * share, len(peers) * boxes[0].shape[1])])

    for n in range(3):
        spread(n).wait_recv()
    total_out[...] = gathered[...]

    for n, (boxes, route) in enumerate(plan):
        for hop in range(3):
            peers = route[hop][0]
            bulk(4 * n + hop, peers, boxes[hop].at[pl.ds(0, len(peers))]).wait_send()
        spread(n).wait_send()
    for b in (1, 2):
        send_query(b).wait_send()
        send_grad(b).wait_send()
    for n in range(4):
        send_lse(n).wait_send()


def run_step(query_lengths, passage_lengths, positives, query_hidden, passage_hidden, projection):
    dma = pltpu.SemaphoreType.DMA
    vmem = pl.BlockSpec(memory_space=pltpu.VMEM)
    hbm = pl.BlockSpec(memory_space=pltpu.HBM)
    vm = pltpu.VMEM
    ny = NYH * NYL
    share = HID // 3
    xa = NX * NC
    return pl.pallas_call(
        step_kernel,
        out_shape=(
            jax.ShapeDtypeStruct((QN,), F32),
            jax.ShapeDtypeStruct((PR + QR, HID), BF16),
            jax.ShapeDtypeStruct((HID, DIM), BF16),
        ),
        in_specs=[hbm] * 6,
        out_specs=(pl.BlockSpec(memory_space=pltpu.SMEM), vmem, vmem),
        scratch_shapes=[
            pltpu.SMEM((QN,), jnp.int32), pltpu.SMEM((PN,), jnp.int32), pltpu.SMEM((QN,), jnp.int32),
            vm((PR + QR, HID), BF16), vm((HID, DIM), BF16),
            vm((3, QR, QR), BF16), vm((DIM, QR), F32), vm((1, QR), F32),
            vm((PR, 2 * DIM), BF16), vm((DIM, PR), BF16), vm((PR, DIM), F32), vm((PR, 1), F32),
            vm((3, PR, QR), F32), vm((3, PR, QR), BF16),
            vm((3, TAIL, QR), F32), vm((3, TAIL, QR), F32), vm((3, TAIL, QR), F32),
            vm((3, TAIL, QR), F32), vm((TAIL, QR), F32), vm((QR, QR), BF16),
            vm((3, 8, QR), F32), vm((4, 8, QR), F32),
            vm((2, DIM, QR), BF16), vm((2, DIM, QR), BF16), vm((2, DIM, QR), BF16),
            vm((PR, DIM), BF16), vm((DIM, PR + QR), BF16),
            vm((PR, DIM), F32), vm((DIM, HID), F32),
            vm((HID, DIM), BF16),
            vm((ny, share // ny, DIM), BF16), vm((NZ, share // ny, DIM), BF16), vm((xa, share // ny, DIM), BF16),
            vm((NZ, share // NZ, DIM), BF16), vm((ny, share // NZ, DIM), BF16), vm((xa, share // NZ, DIM), BF16),
            vm((xa, share // xa, DIM), BF16), vm((ny, share // xa, DIM), BF16), vm((NZ, share // xa, DIM), BF16),
            vm((HID, DIM), BF16),
            dma((6,)), dma((2,)), dma((2,)), dma((4,)), dma((4,)), dma((2,)), dma((2,)),
            dma((12,)), dma((12,)),
        ],
        compiler_params=pltpu.CompilerParams(
            collective_id=0, has_side_effects=True, vmem_limit_bytes=24 * 1024 * 1024),
    )(query_lengths, passage_lengths, positives, query_hidden, passage_hidden, projection)


def finish_kernel(loss, hidden, total, loss_any, gq_any, gp_any, gproj_any, gproj, sem):
    puts = [
        pltpu.make_async_copy(near, far, sem.at[n])
        for n, (near, far) in enumerate((
            (hidden.at[pl.ds(0, PR)], gp_any), (hidden.at[pl.ds(PR, QR)], gq_any),
            (loss, loss_any), (gproj, gproj_any)))]
    for put in puts[:3]:
        put.start()
    for n in range(HID // DIM):
        spot = pl.ds(n * DIM, DIM)
        gproj[spot, :] = total[spot, :].astype(F32).T * (1.0 / (NB * NMP))
    puts[3].start()
    for put in puts:
        put.wait()


def run_finish(loss, hidden, total):
    vmem = pl.BlockSpec(memory_space=pltpu.VMEM)
    hbm = pl.BlockSpec(memory_space=pl.ANY)
    return pl.pallas_call(
        finish_kernel,
        out_shape=(
            jax.ShapeDtypeStruct((QN,), F32),
            jax.ShapeDtypeStruct((QR, HID), BF16),
            jax.ShapeDtypeStruct((PR, HID), BF16),
            jax.ShapeDtypeStruct((HID, DIM), F32),
        ),
        in_specs=[hbm, vmem, vmem],
        out_specs=(hbm, hbm, hbm, hbm),
        scratch_shapes=[pltpu.VMEM((HID, DIM), F32), pltpu.SemaphoreType.DMA((4,))],
        compiler_params=pltpu.CompilerParams(vmem_limit_bytes=16 * 1024 * 1024),
    )(loss, hidden, total)


def per_device(query_hidden, passage_hidden, projection, query_lengths, passage_lengths, positives):
    loss, hidden, total = run_step(*(
        pltpu.with_memory_space_constraint(v, pltpu.HBM) for v in (
            query_lengths, passage_lengths, positives, query_hidden, passage_hidden, projection)))
    return run_finish(loss, hidden, total)


def solution(mesh):
    in_specs = (
        P(("batch", "mp"), None),
        P(("batch", "mp"), None),
        P(),
        P(("batch", "mp")),
        P(("batch", "mp")),
        P(("batch", "mp")),
    )
    out_specs = (P(("batch", "mp")), P(("batch", "mp"), None), P(("batch", "mp"), None), P())
    return jax.shard_map(
        per_device, mesh=mesh, in_specs=in_specs, out_specs=out_specs, check_vma=False
    )
```
